32 devices in a mesh: row: 8 (over y, x, core), col: 4 (over z).
Axes of the slice: x: 2, y: 2, z: 4, core: 2. Of those that a mesh axis runs over, the one named last changes fastest.
Arguments:
- tiles: bfloat16 [128, 64, 128, 128], P('row', 'col'), may hold values from -0.09375 to 0.09375
- col_index: int32 [128, 64], P('row', 'col'), may hold values from 0 to 15
- counts: int32 [128, 4], P('row', 'col'), may hold values from 1 to 16, as said below
- sketch: bfloat16 [8192, 512], P('col'), may hold values from -6 to 6
Outputs:
- basis: float32 [16384, 512], P(('row', 'col'))
- factor: float32 [512, 512], replicated
The draws below stay inside these ranges and needn't reach their ends.
Inputs may be any that keep to these rules, and one draw needn't show every extreme that they name: Slots at or beyond counts hold values that are ignored. Some tile row fills all 16 slots of some ignition block.
All inputs are finite; a program needn't handle non-finite values.
Results may differ from the reference program's by a relative error of at most 0.003.
Values may be sent and summed in bfloat16 or wider, within the bound.
No kernel may reach another device: no remote copies, remote signals or barrier semaphores. Data moves between devices by JAX's collectives and lax.ppermute only.
A program may use at most 128 MiB of HBM per device.

```python
import jax
import jax.numpy as jnp
from jax import lax

TILE = 128
K = 512
SLOT_COUNT = 16
RT = 16
COLUMN_TILES = 16
MT = 128
M = 16384
N = 8192
N_COL = 4


def draw_counts(key, part):
    first, second, third, fourth = jax.random.split(key, 4)
    blocks = MT // RT
    level = jax.random.randint(first, (blocks, 1, 1), 0, 4)
    limit = jnp.maximum(1, SLOT_COUNT * (1 + level) // 4)
    limit = jnp.broadcast_to(limit, (blocks, RT, N_COL)).reshape(MT, N_COL)
    drawn = jax.random.randint(second, (MT, N_COL), 1, limit + 1)
    where_row = jax.random.randint(third, (), 0, MT)
    where_col = jax.random.randint(fourth, (), 0, N_COL)
    return drawn.at[where_row, where_col].set(SLOT_COUNT).astype(jnp.int32)


def place_ends(result, own_key, least, top_value):
    index_at = [jax.random.randint(jax.random.fold_in(own_key, axis), (), 0, length) for axis, length in enumerate(result.shape)]
    widest = result.shape.index(max(result.shape))
    beside = index_at[:widest] + [(index_at[widest] + 1) % result.shape[widest]] + index_at[widest + 1:]
    return result.at[tuple(index_at)].set(least).at[tuple(beside)].set(top_value)


def block_scale(stream_key, shape, cuts, least, top_value):
    loudness = 1.0
    for position, blocks in cuts:
        draws = jax.random.uniform(jax.random.fold_in(jax.random.fold_in(stream_key, 6), position), (blocks,), jnp.float32, least / len(cuts), top_value / len(cuts))
        loudness = loudness * jnp.repeat(jnp.exp(draws), shape[position] // blocks).reshape((-1,) + (1,) * (len(shape) - 1 - position))
    return loudness


def gaussian(own_key, dims, scale, reach, shards=(), kind=jnp.bfloat16):
    level = block_scale(own_key, dims, shards, -0.22, 0.18) if shards else 1.0
    result = jax.random.normal(own_key, dims, jnp.float32) * scale * level
    return jnp.minimum(jnp.maximum(result, -reach), reach).astype(kind)


def setup_inputs(seed: int = 0) -> dict:
    keys = jax.random.split(jax.random.key(seed), 5)
    tiles = gaussian(keys[0], (MT, N_COL * SLOT_COUNT, TILE, TILE), (TILE * SLOT_COUNT * N_COL // 2) ** -0.5, 0.09375, ((0, 8), (1, 4)))
    col_index = place_ends(jax.random.randint(keys[1], (MT, N_COL * SLOT_COUNT), 0, COLUMN_TILES), jax.random.fold_in(keys[1], 1), 0, COLUMN_TILES - 1).astype(jnp.int32)
    counts = draw_counts(jax.random.fold_in(keys[4], 71), 0)
    sketch = gaussian(keys[3], (N, K), 1.0, 6.0, ((0, 4),))
    return dict(tiles=tiles, col_index=col_index, counts=counts, sketch=sketch)


def slot_arrangement(slot_total):
    owning_part = jnp.arange(slot_total) // SLOT_COUNT
    return (owning_part, owning_part * COLUMN_TILES, jnp.arange(slot_total) % SLOT_COUNT)

def forward(tiles, col_index, counts, x_tiles):
    owning_part, offset, within = slot_arrangement(tiles.shape[1])

    def one_row(args):
        tile_row, index_row, count_row = args
        live = (within < count_row[owning_part]).astype(jnp.float32)
        picked = x_tiles[(index_row + offset).astype(jnp.int32)].astype(jnp.float32) * live[:, None, None]
        return jnp.einsum('sab,sbk->ak', tile_row.astype(jnp.float32), picked, precision=lax.Precision.HIGHEST)
    return lax.map(one_row, (tiles, col_index, counts))

def backward(tiles, col_index, counts, q_tiles):
    owning_part, offset, within = slot_arrangement(tiles.shape[1])

    def one_row(total, args):
        tile_row, index_row, count_row, q_row = args
        live = (within < count_row[owning_part]).astype(jnp.float32)
        contribution = jnp.einsum('sab,ak->sbk', tile_row.astype(jnp.float32), q_row.astype(jnp.float32), precision=lax.Precision.HIGHEST)
        contribution = contribution * live[:, None, None]
        return (total.at[(index_row + offset).astype(jnp.int32)].add(contribution), None)
    start = jnp.zeros((N_COL * COLUMN_TILES, TILE, K), jnp.float32)
    total, unused = lax.scan(one_row, start, (tiles, col_index, counts, q_tiles))
    return total

def orthonormal(panel):
    gram = jnp.dot(panel.T.astype(jnp.float32), panel.astype(jnp.float32), precision=lax.Precision.HIGHEST, preferred_element_type=jnp.float32) / M
    lower = jnp.linalg.cholesky(gram)
    basis = lax.linalg.triangular_solve(lower, panel, left_side=False, lower=True, transpose_a=True)
    return (basis, lower.T)

def reference(tiles, col_index, counts, sketch):
    first = forward(tiles, col_index, counts, sketch.reshape(N_COL * COLUMN_TILES, TILE, K)).reshape(M, K)
    first_q, unused = orthonormal(first)
    q_tiles = first_q.astype(jnp.bfloat16).reshape(MT, TILE, K)
    back = backward(tiles, col_index, counts, q_tiles).astype(jnp.bfloat16)
    second = forward(tiles, col_index, counts, back).reshape(M, K)
    basis, factor = orthonormal(second)
    return (basis, factor)
```

```python
import functools

import jax
import jax.numpy as jnp
from jax import lax
from jax.experimental import pallas as pl
from jax.experimental.pallas import tpu as pltpu
from jax.sharding import PartitionSpec as P

HI = lax.Precision.HIGHEST
NT = (((1,), (1,)), ((), ()))
TN = (((0,), (0,)), ((), ()))


def forward_body(group, base, idx_ref, cnt_ref, t_ref, x_ref, o_ref, acc_ref):
    tile = t_ref.shape[2]
    row = pl.program_id(0) + base
    count = cnt_ref[row]
    acc_ref[...] = jnp.zeros_like(acc_ref)

    def step(p, carry):
        lhs, rhs = [], []
        for q in range(group):
            s = p * group + q
            t = t_ref[0, s]
            lhs.append(t if q == 0 else jnp.where(s < count, t, jnp.zeros_like(t)))
            c = pl.multiple_of(idx_ref[row, s] * tile, tile)
            rhs.append(x_ref[pl.ds(c, tile), :])
        acc_ref[...] += jnp.dot(
            jnp.concatenate(lhs, 1), jnp.concatenate(rhs, 0), preferred_element_type=jnp.float32
        )
        return carry

    lax.fori_loop(0, (count + group - 1) // group, step, 0)
    o_ref[...] = acc_ref[...]


def forward(tiles, col_index, counts, x, base, rows):
    slots, tile = tiles.shape[1], tiles.shape[2]
    width = x.shape[1]
    group = next(g for g in (8, 4, 2, 1) if slots % g == 0)
    return pl.pallas_call(
        functools.partial(forward_body, group, base),
        out_shape=jax.ShapeDtypeStruct((rows * tile, width), jnp.float32),
        grid_spec=pltpu.PrefetchScalarGridSpec(
            num_scalar_prefetch=2,
            grid=(rows,),
            in_specs=[
                pl.BlockSpec((1, slots, tile, tile), lambda r, *_: (r + base, 0, 0, 0)),
                pl.BlockSpec(x.shape, lambda r, *_: (0, 0)),
            ],
            out_specs=pl.BlockSpec((tile, width), lambda r, *_: (r, 0)),
            scratch_shapes=[pltpu.VMEM((tile, width), jnp.float32)],
        ),
        name="forward_rows",
    )(col_index, counts, tiles, x)


def backward_body(group, idx_ref, cnt_ref, t_ref, f_ref, z_ref):
    tile = t_ref.shape[2]
    row = pl.program_id(0)
    count = cnt_ref[row]

    @pl.when(row == 0)
    def _():
        z_ref[...] = jnp.zeros_like(z_ref)

    def step(p, carry):
        lhs = []
        for q in range(group):
            s = p * group + q
            t = t_ref[0, s]
            lhs.append(t if q == 0 else jnp.where(s < count, t, jnp.zeros_like(t)))
        out = lax.dot_general(
            jnp.concatenate(lhs, 1), f_ref[...], TN, preferred_element_type=jnp.float32
        )
        for q in range(group):
            c = pl.multiple_of(idx_ref[row, p * group + q] * tile, tile)
            z_ref[pl.ds(c, tile), :] += out[q * tile:(q + 1) * tile]
        return carry

    lax.fori_loop(0, (count + group - 1) // group, step, 0)


def backward(tiles, col_index, counts, panel, col_rows):
    rows, slots, tile = tiles.shape[:3]
    width = panel.shape[1]
    group = next(g for g in (4, 2, 1) if slots % g == 0)
    return pl.pallas_call(
        functools.partial(backward_body, group),
        out_shape=jax.ShapeDtypeStruct((col_rows, width), jnp.float32),
        grid_spec=pltpu.PrefetchScalarGridSpec(
            num_scalar_prefetch=2,
            grid=(rows,),
            in_specs=[
                pl.BlockSpec((1, slots, tile, tile), lambda r, *_: (r, 0, 0, 0)),
                pl.BlockSpec((tile, width), lambda r, *_: (r, 0)),
            ],
            out_specs=pl.BlockSpec((col_rows, width), lambda r, *_: (0, 0)),
        ),
        name="backward_rows",
    )(col_index, counts, tiles, panel)


def factor_block(read, r_ref, t_ref, group):
    n = 128
    vr = n // 8
    a = [read(v) for v in range(vr)]
    lane = lax.broadcasted_iota(jnp.int32, (8, n), 1)
    sub = lax.broadcasted_iota(jnp.int32, (8, n), 0)
    e = [(lane == sub + 8 * v).astype(jnp.float32) for v in range(vr)]
    full = lambda x: jnp.broadcast_to(x, (8, n))
    for g in range(n // group):
        j0 = g * group
        v0, o = j0 // 8, j0 % 8
        P = [full(a[v0][o + k:o + k + 1, :]) for k in range(group)]
        PE = [full(e[v0][o + k:o + k + 1, :]) for k in range(group)]
        el = [[full(P[i][:, j0 + k:j0 + k + 1]) for k in range(i + 1)] for i in range(group)]
        vs = [v for v in range(vr) if v > v0 or (v == v0 and o + group < 8)]
        mult = {v: [full(a[v][:, j0 + k:j0 + k + 1]) for k in range(group)] for v in vs}
        R, RE, S = [], [], []
        W = [None] * group
        WE = [None] * group
        L = [[None] * group for _ in range(group)]
        for c in range(group):
            inv = lax.rsqrt(el[c][c])
            for i in range(c + 1, group):
                L[i][c] = el[i][c] * inv
            for i in range(c + 1, group):
                for k in range(c + 1, i + 1):
                    el[i][k] = el[i][k] - L[i][c] * L[k][c]
            s = []
            for k in range(c):
                t = L[c][k] * S[k][k]
                for j in range(k + 1, c):
                    t = t + L[c][j] * S[j][k]
                s.append(-(t * inv))
            s.append(inv)
            S.append(s)
            r = P[c] * s[c]
            re = PE[c] * s[c]
            for k in range(c):
                r = r + P[k] * s[k]
                re = re + PE[k] * s[k]
            R.append(r); RE.append(re)
            for k in range(c + 1):
                W[k] = s[k] * r if W[k] is None else W[k] + s[k] * r
                WE[k] = s[k] * re if WE[k] is None else WE[k] + s[k] * re
            r_ref[j0 + c:j0 + c + 1, :] = r[0:1, :]
            t_ref[j0 + c:j0 + c + 1, :] = re[0:1, :]
        for v in vs:
            u = mult[v][0] * W[0]
            ue = mult[v][0] * WE[0]
            for k in range(1, group):
                u = u + mult[v][k] * W[k]
                ue = ue + mult[v][k] * WE[k]
            a[v] = a[v] - u
            e[v] = e[v] - ue


def chol_body(scale, group, g_ref, r_ref, t_ref, a_ref, rk_ref, tk_ref):
    n = g_ref.shape[0]
    b = 128
    a_ref[...] = g_ref[...] * scale
    rows = lax.broadcasted_iota(jnp.int32, (n, n), 0)
    cols = lax.broadcasted_iota(jnp.int32, (n, n), 1)
    t_ref[...] = jnp.where(rows == cols, 1.0, 0.0).astype(jnp.float32)

    def block(k, carry):
        at = pl.multiple_of(k * b, b)
        factor_block(lambda v: a_ref[pl.ds(pl.multiple_of(at + 8 * v, 8), 8), pl.ds(at, b)], rk_ref, tk_ref, group)
        inv = tk_ref[...]
        rp = jnp.dot(inv, a_ref[pl.ds(at, b), :], precision=HI, preferred_element_type=jnp.float32)
        ep = jnp.dot(inv, t_ref[pl.ds(at, b), :], precision=HI, preferred_element_type=jnp.float32)
        row = lax.broadcasted_iota(jnp.int32, rp.shape, 0) + at
        col = lax.broadcasted_iota(jnp.int32, rp.shape, 1)
        r_ref[pl.ds(at, b), :] = jnp.where(col >= row, rp, 0.0)
        t_ref[pl.ds(at, b), :] = jnp.where(col <= row, ep, 0.0)

        def below(i, carry):
            to = pl.multiple_of(i * b, b)
            l = r_ref[pl.ds(at, b), pl.ds(to, b)]
            a_ref[pl.ds(to, b), :] -= lax.dot_general(l, r_ref[pl.ds(at, b), :], TN, precision=HI, preferred_element_type=jnp.float32)
            t_ref[pl.ds(to, b), :] -= lax.dot_general(l, t_ref[pl.ds(at, b), :], TN, precision=HI, preferred_element_type=jnp.float32)
            return carry
        lax.fori_loop(k + 1, n // b, below, 0)
        return carry
    lax.fori_loop(0, n // b, block, 0)


def cholesky(gram, scale, group=8):
    n = gram.shape[0]
    s = jax.ShapeDtypeStruct((n, n), jnp.float32)
    return pl.pallas_call(
        functools.partial(chol_body, scale, group),
        out_shape=(s, s),
        scratch_shapes=[pltpu.VMEM((n, n), jnp.float32), pltpu.VMEM((128, 128), jnp.float32), pltpu.VMEM((128, 128), jnp.float32)],
        name="factorize",
    )(gram)


def line_sum(value, wire):
    n = lax.axis_size("col")
    z = lax.axis_index("col")
    for s in range(n // 2 - 1):
        pairs = [(s, s + 1), (n - 1 - s, n - 2 - s)]
        value = value + lax.ppermute(value.astype(wire), "col", pairs).astype(value.dtype)
    pairs = [(n // 2 - 1, n // 2), (n // 2, n // 2 - 1)]
    value = value + lax.ppermute(value.astype(wire), "col", pairs).astype(value.dtype)
    value = value.astype(wire)
    for s in reversed(range(n // 2 - 1)):
        pairs = [(s + 1, s), (n - 2 - s, n - 1 - s)]
        got = lax.ppermute(value, "col", pairs)
        value = jnp.where((z == s) | (z == n - 1 - s), got, value)
    return value


def halving(bits):
    size = 2**bits
    me = lax.axis_index("row")
    odd = me & 1
    for step in range(bits):
        even_bit = step
        odd_bit = 0 if step == 0 else bits - step
        pairs = [(i, i ^ (1 << (odd_bit if i & 1 else even_bit))) for i in range(size)]
        own = jnp.where(odd == 1, (me >> odd_bit) & 1, (me >> even_bit) & 1)
        yield pairs, own


def row_scatter(value, wires):
    bits = lax.axis_size("row").bit_length() - 1
    offset = jnp.int32(0)
    for step, (pairs, own) in enumerate(halving(bits)):
        half = value.shape[0] // 2
        give = lax.dynamic_slice_in_dim(value, (1 - own) * half, half, 0).astype(wires[min(step, len(wires) - 1)])
        keep = lax.dynamic_slice_in_dim(value, own * half, half, 0)
        value = keep + lax.ppermute(give, "row", pairs).astype(value.dtype)
        offset = offset + own * half
    return value, offset


def row_gather(part, offset, total):
    bits = lax.axis_size("row").bit_length() - 1
    steps = list(halving(bits))
    for pairs, own in reversed(steps):
        got = lax.ppermute(part, "row", pairs)
        low = jnp.where(own == 0, part, got)
        high = jnp.where(own == 0, got, part)
        part = jnp.concatenate([low, high], 0)
    return part


def gram_sum(gram):
    part, offset = row_scatter(gram, (jnp.float32,))
    part = line_sum(part, jnp.float32)
    return row_gather(part, offset, gram.shape[0])


def line_scatter(value):
    n = lax.axis_size("col")
    z = lax.axis_index("col")
    share = value.shape[0] // n

    def own(q):
        return lax.dynamic_slice_in_dim(value, jnp.clip(q, 0, n - 1) * share, share, 0)

    right = left = None
    for t in range(1, n):
        up = own(n - 1 - (t - 1 - z))
        down = own(t - 1 - (n - 1 - z))
        if right is not None:
            up = up + right.astype(up.dtype)
            down = down + left.astype(down.dtype)
        wire = jnp.float32 if t == n - 1 else jnp.bfloat16
        right = lax.ppermute(up.astype(wire), "col", [(i, i + 1) for i in range(t)])
        left = lax.ppermute(down.astype(wire), "col", [(n - 1 - i, n - 2 - i) for i in range(t)])
    return own(z) + right.astype(value.dtype) + left.astype(value.dtype)


def local(tiles, col_index, counts, sketch):
    tile_rows, slots, tile = tiles.shape[:3]
    n_col = lax.axis_size("col")
    total_rows = tile_rows * tile * lax.axis_size("row")
    counts = counts.reshape(-1)
    z = lax.axis_index("col")

    chunk = tile_rows // n_col
    firsts = []
    for j in range(n_col):
        part = forward(tiles, col_index, counts, sketch, j * chunk, chunk)
        firsts.append(line_sum(part, jnp.bfloat16))
    first = jnp.concatenate(firsts, 0)

    share = first.shape[0] // n_col
    mine = lax.dynamic_slice_in_dim(first, z * share, share, 0)
    gram = lax.dot_general(mine, mine, TN, preferred_element_type=jnp.float32)
    unused, inverse = cholesky(gram_sum(gram), 1.0 / total_rows)

    back = backward(tiles, col_index, counts, first, sketch.shape[0])
    part, offset = row_scatter(back, (jnp.float32, jnp.bfloat16, jnp.float32))
    part = lax.dot_general(part, inverse, NT, precision=HI, preferred_element_type=jnp.float32)
    back = row_gather(part.astype(jnp.bfloat16), offset, sketch.shape[0])

    second = line_scatter(forward(tiles, col_index, counts, back, 0, tile_rows))
    gram = lax.dot_general(second, second, TN, precision=HI, preferred_element_type=jnp.float32)
    factor, inverse = cholesky(gram_sum(gram), 1.0 / total_rows)
    basis = lax.dot_general(second, inverse, NT, precision=HI, preferred_element_type=jnp.float32)
    return (basis, factor)


def solution(mesh):
    return jax.shard_map(
        local,
        mesh=mesh,
        in_specs=(P("row", "col", None, None), P("row", "col"), P("row", "col"), P("col", None)),
        out_specs=(P(("row", "col"), None), P()),
        check_vma=False,
    )
```

```python
import functools

import jax
import jax.numpy as jnp
from jax import lax
from jax.experimental import pallas as pl
from jax.experimental.pallas import tpu as pltpu
from jax.sharding import PartitionSpec as P

HI = lax.Precision.HIGHEST
NT = (((1,), (1,)), ((), ()))
TN = (((0,), (0,)), ((), ()))


def forward_body(group, base_ref, idx_ref, cnt_ref, t_ref, x_ref, o_ref, acc_ref):
    tile = t_ref.shape[2]
    row = pl.program_id(0) + base_ref[0]
    count = cnt_ref[row]
    acc_ref[...] = jnp.zeros_like(acc_ref)

    def step(p, carry):
        lhs, rhs = [], []
        for q in range(group):
            s = p * group + q
            t = t_ref[0, s]
            lhs.append(t if q == 0 else jnp.where(s < count, t, jnp.zeros_like(t)))
            c = pl.multiple_of(idx_ref[row, s] * tile, tile)
            rhs.append(x_ref[pl.ds(c, tile), :])
        acc_ref[...] += jnp.dot(
            jnp.concatenate(lhs, 1), jnp.concatenate(rhs, 0), preferred_element_type=jnp.float32
        )
        return carry

    lax.fori_loop(0, (count + group - 1) // group, step, 0)
    o_ref[...] = acc_ref[...]


def forward(tiles, col_index, counts, x, base, rows):
    slots, tile = tiles.shape[1], tiles.shape[2]
    width = x.shape[1]
    group = next(g for g in (8, 4, 2, 1) if slots % g == 0)
    return pl.pallas_call(
        functools.partial(forward_body, group),
        out_shape=jax.ShapeDtypeStruct((rows * tile, width), jnp.float32),
        grid_spec=pltpu.PrefetchScalarGridSpec(
            num_scalar_prefetch=3,
            grid=(rows,),
            in_specs=[
                pl.BlockSpec((1, slots, tile, tile), lambda r, at, *_: (r + at[0], 0, 0, 0)),
                pl.BlockSpec(x.shape, lambda r, *_: (0, 0)),
            ],
            out_specs=pl.BlockSpec((tile, width), lambda r, *_: (r, 0)),
            scratch_shapes=[pltpu.VMEM((tile, width), jnp.float32)],
        ),
        name="forward_rows",
    )(jnp.full((1,), base, jnp.int32), col_index, counts, tiles, x)


def backward_body(group, base, first, idx_ref, cnt_ref, t_ref, f_ref, *refs):
    z_ref = refs[-1]
    tile = t_ref.shape[2]
    row = pl.program_id(0) + base
    count = cnt_ref[row]

    @pl.when(pl.program_id(0) == 0)
    def _():
        z_ref[...] = jnp.zeros_like(z_ref) if first else refs[0][...]

    def step(p, carry):
        lhs = []
        for q in range(group):
            s = p * group + q
            t = t_ref[0, s]
            lhs.append(t if q == 0 else jnp.where(s < count, t, jnp.zeros_like(t)))
        out = lax.dot_general(
            jnp.concatenate(lhs, 1), f_ref[...], TN, preferred_element_type=jnp.float32
        )
        for q in range(group):
            c = pl.multiple_of(idx_ref[row, p * group + q] * tile, tile)
            z_ref[pl.ds(c, tile), :] += out[q * tile:(q + 1) * tile]
        return carry

    lax.fori_loop(0, (count + group - 1) // group, step, 0)


def backward(tiles, col_index, counts, panel, col_rows, base, total):
    slots, tile = tiles.shape[1], tiles.shape[2]
    width = panel.shape[1]
    group = next(g for g in (4, 2, 1) if slots % g == 0)
    whole = pl.BlockSpec((col_rows, width), lambda r, *_: (0, 0), pipeline_mode=pl.Buffered(1))
    more = () if total is None else (total,)
    return pl.pallas_call(
        functools.partial(backward_body, group, base, total is None),
        out_shape=jax.ShapeDtypeStruct((col_rows, width), jnp.float32),
        grid_spec=pltpu.PrefetchScalarGridSpec(
            num_scalar_prefetch=2,
            grid=(panel.shape[0] // tile,),
            in_specs=[
                pl.BlockSpec((1, slots, tile, tile), lambda r, *_: (r + base, 0, 0, 0)),
                pl.BlockSpec((tile, width), lambda r, *_: (r, 0)),
            ] + [whole] * len(more),
            out_specs=pl.BlockSpec((col_rows, width), lambda r, *_: (0, 0)),
        ),
        name="backward_rows",
    )(col_index, counts, tiles, panel, *more)


def factor_block(read, r_ref, t_ref, group):
    n = 128
    vr = n // 8
    a = [read(v) for v in range(vr)]
    lane = lax.broadcasted_iota(jnp.int32, (8, n), 1)
    sub = lax.broadcasted_iota(jnp.int32, (8, n), 0)
    e = [(lane == sub + 8 * v).astype(jnp.float32) for v in range(vr)]
    full = lambda x: jnp.broadcast_to(x, (8, n))
    for g in range(n // group):
        j0 = g * group
        v0, o = j0 // 8, j0 % 8
        P = [full(a[v0][o + k:o + k + 1, :]) for k in range(group)]
        PE = [full(e[v0][o + k:o + k + 1, :]) for k in range(group)]
        el = [[full(P[i][:, j0 + k:j0 + k + 1]) for k in range(i + 1)] for i in range(group)]
        vs = [v for v in range(vr) if v > v0 or (v == v0 and o + group < 8)]
        mult = {v: [full(a[v][:, j0 + k:j0 + k + 1]) for k in range(group)] for v in vs}
        R, RE, S = [], [], []
        W = [None] * group
        WE = [None] * group
        L = [[None] * group for _ in range(group)]
        for c in range(group):
            inv = lax.rsqrt(el[c][c])
            for i in range(c + 1, group):
                L[i][c] = el[i][c] * inv
            for i in range(c + 1, group):
                for k in range(c + 1, i + 1):
                    el[i][k] = el[i][k] - L[i][c] * L[k][c]
            s = []
            for k in range(c):
                t = L[c][k] * S[k][k]
                for j in range(k + 1, c):
                    t = t + L[c][j] * S[j][k]
                s.append(-(t * inv))
            s.append(inv)
            S.append(s)
            r = P[c] * s[c]
            re = PE[c] * s[c]
            for k in range(c):
                r = r + P[k] * s[k]
                re = re + PE[k] * s[k]
            R.append(r); RE.append(re)
            for k in range(c + 1):
                W[k] = s[k] * r if W[k] is None else W[k] + s[k] * r
                WE[k] = s[k] * re if WE[k] is None else WE[k] + s[k] * re
            r_ref[j0 + c:j0 + c + 1, :] = r[0:1, :]
            t_ref[j0 + c:j0 + c + 1, :] = re[0:1, :]
        for v in vs:
            u = mult[v][0] * W[0]
            ue = mult[v][0] * WE[0]
            for k in range(1, group):
                u = u + mult[v][k] * W[k]
                ue = ue + mult[v][k] * WE[k]
            a[v] = a[v] - u
            e[v] = e[v] - ue


def chol_body(scale, group, g_ref, r_ref, t_ref, a_ref, rk_ref, tk_ref):
    n = g_ref.shape[0]
    b = 128
    a_ref[...] = g_ref[...] * scale
    rows = lax.broadcasted_iota(jnp.int32, (n, n), 0)
    cols = lax.broadcasted_iota(jnp.int32, (n, n), 1)
    t_ref[...] = jnp.where(rows == cols, 1.0, 0.0).astype(jnp.float32)

    def block(k, carry):
        at = pl.multiple_of(k * b, b)
        factor_block(lambda v: a_ref[pl.ds(pl.multiple_of(at + 8 * v, 8), 8), pl.ds(at, b)], rk_ref, tk_ref, group)
        inv = tk_ref[...]
        rp = jnp.dot(inv, a_ref[pl.ds(at, b), :], precision=HI, preferred_element_type=jnp.float32)
        ep = jnp.dot(inv, t_ref[pl.ds(at, b), :], precision=HI, preferred_element_type=jnp.float32)
        row = lax.broadcasted_iota(jnp.int32, rp.shape, 0) + at
        col = lax.broadcasted_iota(jnp.int32, rp.shape, 1)
        r_ref[pl.ds(at, b), :] = jnp.where(col >= row, rp, 0.0)
        t_ref[pl.ds(at, b), :] = jnp.where(col <= row, ep, 0.0)

        def below(i, carry):
            to = pl.multiple_of(i * b, b)
            l = r_ref[pl.ds(at, b), pl.ds(to, b)]
            a_ref[pl.ds(to, b), :] -= lax.dot_general(l, r_ref[pl.ds(at, b), :], TN, precision=HI, preferred_element_type=jnp.float32)
            t_ref[pl.ds(to, b), :] -= lax.dot_general(l, t_ref[pl.ds(at, b), :], TN, precision=HI, preferred_element_type=jnp.float32)
            return carry
        lax.fori_loop(k + 1, n // b, below, 0)
        return carry
    lax.fori_loop(0, n // b, block, 0)


def cholesky(gram, scale, group=8):
    n = gram.shape[0]
    s = jax.ShapeDtypeStruct((n, n), jnp.float32)
    return pl.pallas_call(
        functools.partial(chol_body, scale, group),
        out_shape=(s, s),
        scratch_shapes=[pltpu.VMEM((n, n), jnp.float32), pltpu.VMEM((128, 128), jnp.float32), pltpu.VMEM((128, 128), jnp.float32)],
        name="factorize",
    )(gram)


def line_inward(value, wire):
    n = lax.axis_size("col")
    got = jnp.zeros_like(value).astype(wire)
    for s in range(n // 2 - 1):
        if s:
            value = value + got.astype(value.dtype)
        got = lax.ppermute(value.astype(wire), "col", [(s, s + 1), (n - 1 - s, n - 2 - s)])
    return value, got


def line_across(value, wire):
    n = lax.axis_size("col")
    pairs = [(n // 2 - 1, n // 2), (n // 2, n // 2 - 1)]
    return (value + lax.ppermute(value.astype(wire), "col", pairs).astype(value.dtype)).astype(wire)


def line_outward(value, beside=None):
    n = lax.axis_size("col")
    z = lax.axis_index("col")
    for s in reversed(range(n // 2 - 1)):
        pairs = [(s + 1, s), (n - 2 - s, n - 1 - s)]
        got = lax.ppermute(value, "col", pairs)
        if beside is not None:
            value, beside = lax.optimization_barrier((value, beside))
        value = jnp.where((z == s) | (z == n - 1 - s), got, value)
    return value, beside


def col_sum(value):
    n = lax.axis_size("col")
    for bit in range(n.bit_length() - 1):
        value = value + lax.ppermute(value, "col", [(i, i ^ (1 << bit)) for i in range(n)])
    return value


def halving(bits):
    size = 2**bits
    me = lax.axis_index("row")
    odd = me & 1
    for step in range(bits):
        even_bit = step
        odd_bit = 0 if step == 0 else bits - step
        pairs = [(i, i ^ (1 << (odd_bit if i & 1 else even_bit))) for i in range(size)]
        own = jnp.where(odd == 1, (me >> odd_bit) & 1, (me >> even_bit) & 1)
        yield pairs, own


def row_scatter(value, wires):
    bits = lax.axis_size("row").bit_length() - 1
    offset = jnp.int32(0)
    for step, (pairs, own) in enumerate(halving(bits)):
        half = value.shape[0] // 2
        give = lax.dynamic_slice_in_dim(value, (1 - own) * half, half, 0).astype(wires[min(step, len(wires) - 1)])
        keep = lax.dynamic_slice_in_dim(value, own * half, half, 0)
        value = keep + lax.ppermute(give, "row", pairs).astype(value.dtype)
        offset = offset + own * half
    return value, offset


def row_gather(part, offset, total):
    bits = lax.axis_size("row").bit_length() - 1
    steps = list(halving(bits))
    for pairs, own in reversed(steps):
        got = lax.ppermute(part, "row", pairs)
        low = jnp.where(own == 0, part, got)
        high = jnp.where(own == 0, got, part)
        part = jnp.concatenate([low, high], 0)
    return part


def gram_sum(gram):
    part, offset = row_scatter(gram, (jnp.float32,))
    part = col_sum(part)
    return row_gather(part, offset, gram.shape[0])


def share_order(k):
    n = lax.axis_size("col")
    z = lax.axis_index("col")
    low = jnp.where(k < n - 1 - z, n - 1 - k, k - (n - 1 - z))
    high = jnp.where(k < z, k, n - 1 - (k - z))
    return jnp.where(k == n - 1, z, jnp.where(z < n // 2, low, high))


def line_scatter(parts):
    n = lax.axis_size("col")
    z = lax.axis_index("col")

    def pick(t, lag):
        value = parts[t - 1]
        for d in range(1, min(n // 2, t)):
            value = jnp.where(lag == d, parts[t - 1 - d], value)
        return value

    right = left = None
    for t in range(1, n):
        up = pick(t, jnp.where(z < n // 2, z, 0))
        down = pick(t, jnp.where(z < n // 2, 0, n - 1 - z))
        if right is not None:
            up = up + right.astype(up.dtype)
            down = down + left.astype(down.dtype)
        wire = jnp.float32 if t == n - 1 else jnp.bfloat16
        right = lax.ppermute(up.astype(wire), "col", [(i, i + 1) for i in range(t)])
        left = lax.ppermute(down.astype(wire), "col", [(n - 1 - i, n - 2 - i) for i in range(t)])
        right, left = lax.optimization_barrier((right, left))
    return parts[n - 1] + right.astype(jnp.float32) + left.astype(jnp.float32)


def local(tiles, col_index, counts, sketch):
    tile_rows, slots, tile = tiles.shape[:3]
    n_col = lax.axis_size("col")
    total_rows = tile_rows * tile * lax.axis_size("row")
    counts = counts.reshape(-1)
    z = lax.axis_index("col")

    chunk = tile_rows // n_col
    halves, sums, sent = [], [], []
    for j in range(n_col):
        live = counts
        if j >= 2:
            live, halves[j - 2] = lax.optimization_barrier((counts, halves[j - 2]))
        part = forward(tiles, col_index, live, sketch, j * chunk, chunk)
        if j >= 1:
            value, got = sent[j - 1]
            value, part = lax.optimization_barrier((value, part))
            halves.append(value + got.astype(value.dtype))
        sent.append(line_inward(part, jnp.bfloat16))
    value, got = sent[-1]
    halves.append(value + got.astype(value.dtype))
    crossed = [line_across(half, jnp.bfloat16) for half in halves]
    back = None
    for j in range(n_col):
        total, back = line_outward(crossed[j], back)
        sums.append(total)
        if j < n_col - 1:
            back = backward(tiles, col_index, counts, total, sketch.shape[0], j * chunk, back)
    first = jnp.concatenate(sums, 0)

    share = first.shape[0] // n_col
    mine = lax.dynamic_slice_in_dim(first, z * share, share, 0)
    gram = lax.dot_general(mine, mine, TN, preferred_element_type=jnp.float32)
    unused, inverse = cholesky(gram_sum(gram), 1.0 / total_rows)

    back = backward(tiles, col_index, counts, sums[-1], sketch.shape[0], (n_col - 1) * chunk, back)
    part, offset = row_scatter(back, (jnp.float32, jnp.bfloat16, jnp.float32))
    part = lax.dot_general(part, inverse, NT, precision=HI, preferred_element_type=jnp.float32)
    back = row_gather(part.astype(jnp.bfloat16), offset, sketch.shape[0])

    parts = [
        forward(tiles, col_index, counts, back, share_order(k) * chunk, chunk) for k in range(n_col)
    ]
    second = line_scatter(parts)
    gram = lax.dot_general(second, second, TN, precision=HI, preferred_element_type=jnp.float32)
    factor, inverse = cholesky(gram_sum(gram), 1.0 / total_rows)
    basis = lax.dot_general(second, inverse, NT, precision=HI, preferred_element_type=jnp.float32)
    return (basis, factor)


def solution(mesh):
    return jax.shard_map(
        local,
        mesh=mesh,
        in_specs=(P("row", "col", None, None), P("row", "col"), P("row", "col"), P("col", None)),
        out_specs=(P(("row", "col"), None), P()),
        check_vma=False,
    )
```

```python
import functools

import jax
import jax.numpy as jnp
from jax import lax
from jax.experimental import pallas as pl
from jax.experimental.pallas import tpu as pltpu
from jax.sharding import PartitionSpec as P

HI = lax.Precision.HIGHEST
NT = (((1,), (1,)), ((), ()))
TN = (((0,), (0,)), ((), ()))


def forward_body(group, base_ref, idx_ref, cnt_ref, t_ref, x_ref, o_ref, acc_ref):
    tile = t_ref.shape[2]
    row = pl.program_id(0) + base_ref[0]
    count = cnt_ref[row]
    acc_ref[...] = jnp.zeros_like(acc_ref)

    def step(p, carry):
        lhs, rhs = [], []
        for q in range(group):
            s = p * group + q
            t = t_ref[0, s]
            lhs.append(t if q == 0 else jnp.where(s < count, t, jnp.zeros_like(t)))
            c = pl.multiple_of(idx_ref[row, s] * tile, tile)
            rhs.append(x_ref[pl.ds(c, tile), :])
        acc_ref[...] += jnp.dot(
            jnp.concatenate(lhs, 1), jnp.concatenate(rhs, 0), preferred_element_type=jnp.float32
        )
        return carry

    lax.fori_loop(0, (count + group - 1) // group, step, 0)
    o_ref[...] = acc_ref[...]


def forward(tiles, col_index, counts, x, base, rows):
    slots, tile = tiles.shape[1], tiles.shape[2]
    width = x.shape[1]
    group = next(g for g in (8, 4, 2, 1) if slots % g == 0)
    return pl.pallas_call(
        functools.partial(forward_body, group),
        out_shape=jax.ShapeDtypeStruct((rows * tile, width), jnp.float32),
        grid_spec=pltpu.PrefetchScalarGridSpec(
            num_scalar_prefetch=3,
            grid=(rows,),
            in_specs=[
                pl.BlockSpec((1, slots, tile, tile), lambda r, at, *_: (r + at[0], 0, 0, 0)),
                pl.BlockSpec(x.shape, lambda r, *_: (0, 0)),
            ],
            out_specs=pl.BlockSpec((tile, width), lambda r, *_: (r, 0)),
            scratch_shapes=[pltpu.VMEM((tile, width), jnp.float32)],
        ),
        name="forward_rows",
    )(jnp.full((1,), base, jnp.int32), col_index, counts, tiles, x)


def backward_body(group, base, panels, idx_ref, cnt_ref, t_ref, *refs):
    z_ref = refs[-1]
    tile = t_ref.shape[2]
    at = pl.program_id(0)
    each = pl.num_programs(0) // panels
    row = at + base
    count = cnt_ref[row]
    f = refs[0][...]
    for k in range(1, panels):
        f = jnp.where(at >= k * each, refs[k][...], f)

    @pl.when(at == 0)
    def _():
        z_ref[...] = refs[panels][...] if len(refs) > panels + 1 else jnp.zeros_like(z_ref)

    def step(p, carry):
        lhs = []
        for q in range(group):
            s = p * group + q
            t = t_ref[0, s]
            lhs.append(t if q == 0 else jnp.where(s < count, t, jnp.zeros_like(t)))
        out = lax.dot_general(
            jnp.concatenate(lhs, 1), f, TN, preferred_element_type=jnp.float32
        )
        for q in range(group):
            c = pl.multiple_of(idx_ref[row, p * group + q] * tile, tile)
            z_ref[pl.ds(c, tile), :] += out[q * tile:(q + 1) * tile]
        return carry

    lax.fori_loop(0, (count + group - 1) // group, step, 0)


def backward(tiles, col_index, counts, panels, col_rows, base, total):
    slots, tile = tiles.shape[1], tiles.shape[2]
    width = panels[0].shape[1]
    each = panels[0].shape[0] // tile
    group = next(g for g in (4, 2, 1) if slots % g == 0)
    whole = pl.BlockSpec((col_rows, width), lambda r, *_: (0, 0), pipeline_mode=pl.Buffered(1))
    more = () if total is None else (total,)

    def panel_map(k):
        return lambda r, *_: (jnp.clip(r - k * each, 0, each - 1), 0)

    return pl.pallas_call(
        functools.partial(backward_body, group, base, len(panels)),
        out_shape=jax.ShapeDtypeStruct((col_rows, width), jnp.float32),
        grid_spec=pltpu.PrefetchScalarGridSpec(
            num_scalar_prefetch=2,
            grid=(each * len(panels),),
            in_specs=[pl.BlockSpec((1, slots, tile, tile), lambda r, *_: (r + base, 0, 0, 0))]
            + [pl.BlockSpec((tile, width), panel_map(k)) for k in range(len(panels))]
            + [whole] * len(more),
            out_specs=pl.BlockSpec((col_rows, width), lambda r, *_: (0, 0)),
        ),
        name="backward_rows",
    )(col_index, counts, tiles, *panels, *more)


def factor_block(read, r_ref, t_ref, group):
    n = 128
    vr = n // 8
    a = [read(v) for v in range(vr)]
    lane = lax.broadcasted_iota(jnp.int32, (8, n), 1)
    sub = lax.broadcasted_iota(jnp.int32, (8, n), 0)
    e = [(lane == sub + 8 * v).astype(jnp.float32) for v in range(vr)]
    full = lambda x: jnp.broadcast_to(x, (8, n))
    for g in range(n // group):
        j0 = g * group
        v0, o = j0 // 8, j0 % 8
        P = [full(a[v0][o + k:o + k + 1, :]) for k in range(group)]
        PE = [full(e[v0][o + k:o + k + 1, :]) for k in range(group)]
        el = [[full(P[i][:, j0 + k:j0 + k + 1]) for k in range(i + 1)] for i in range(group)]
        vs = [v for v in range(vr) if v > v0 or (v == v0 and o + group < 8)]
        mult = {v: [full(a[v][:, j0 + k:j0 + k + 1]) for k in range(group)] for v in vs}
        R, RE, S = [], [], []
        W = [None] * group
        WE = [None] * group
        L = [[None] * group for _ in range(group)]
        for c in range(group):
            inv = lax.rsqrt(el[c][c])
            for i in range(c + 1, group):
                L[i][c] = el[i][c] * inv
            for i in range(c + 1, group):
                for k in range(c + 1, i + 1):
                    el[i][k] = el[i][k] - L[i][c] * L[k][c]
            s = []
            for k in range(c):
                t = L[c][k] * S[k][k]
                for j in range(k + 1, c):
                    t = t + L[c][j] * S[j][k]
                s.append(-(t * inv))
            s.append(inv)
            S.append(s)
            r = P[c] * s[c]
            re = PE[c] * s[c]
            for k in range(c):
                r = r + P[k] * s[k]
                re = re + PE[k] * s[k]
            R.append(r); RE.append(re)
            for k in range(c + 1):
                W[k] = s[k] * r if W[k] is None else W[k] + s[k] * r
                WE[k] = s[k] * re if WE[k] is None else WE[k] + s[k] * re
            r_ref[j0 + c:j0 + c + 1, :] = r[0:1, :]
            t_ref[j0 + c:j0 + c + 1, :] = re[0:1, :]
        for v in vs:
            u = mult[v][0] * W[0]
            ue = mult[v][0] * WE[0]
            for k in range(1, group):
                u = u + mult[v][k] * W[k]
                ue = ue + mult[v][k] * WE[k]
            a[v] = a[v] - u
            e[v] = e[v] - ue


def chol_body(scale, group, g_ref, r_ref, t_ref, w_ref, rk_ref, tk_ref):
    n = g_ref.shape[0]
    b = 128
    w_ref[...] = g_ref[...] * scale

    def block(k, carry):
        at = pl.multiple_of(k * b, b)

        def read(v):
            return w_ref[pl.ds(pl.multiple_of(at + 8 * v, 8), 8), pl.ds(at, b)]

        factor_block(read, rk_ref, tk_ref, group)
        inv = tk_ref[...]
        x = jnp.dot(inv, w_ref[pl.ds(at, b), :], precision=HI, preferred_element_type=jnp.float32)
        row = lax.broadcasted_iota(jnp.int32, x.shape, 0) + at
        col = lax.broadcasted_iota(jnp.int32, x.shape, 1)
        r_ref[pl.ds(at, b), :] = jnp.where(col >= at + b, x, 0.0)
        r_ref[pl.ds(at, b), pl.ds(at, b)] = jnp.where(
            col[:, :b] >= row[:, :b] - at, rk_ref[...], 0.0
        )
        inv = jnp.where(col[:, :b] <= row[:, :b] - at, inv, 0.0)
        t_ref[pl.ds(at, b), :] = jnp.where(col < at, x, 0.0)
        t_ref[pl.ds(at, b), pl.ds(at, b)] = inv
        w_ref[pl.ds(at, b), :] = x
        w_ref[pl.ds(at, b), pl.ds(at, b)] = inv

        def below(i, carry):
            to = pl.multiple_of(i * b, b)
            l = r_ref[pl.ds(at, b), pl.ds(to, b)]
            w_ref[pl.ds(to, b), pl.ds(at, b)] = jnp.zeros((b, b), jnp.float32)
            w_ref[pl.ds(to, b), :] -= lax.dot_general(
                l, w_ref[pl.ds(at, b), :], TN, precision=HI, preferred_element_type=jnp.float32
            )
            return carry

        lax.fori_loop(k + 1, n // b, below, 0)
        return carry

    lax.fori_loop(0, n // b, block, 0)


def cholesky(gram, scale, group=8):
    n = gram.shape[0]
    s = jax.ShapeDtypeStruct((n, n), jnp.float32)
    return pl.pallas_call(
        functools.partial(chol_body, scale, group),
        out_shape=(s, s),
        scratch_shapes=[
            pltpu.VMEM((n, n), jnp.float32),
            pltpu.VMEM((128, 128), jnp.float32),
            pltpu.VMEM((128, 128), jnp.float32),
        ],
        name="factorize",
    )(gram)


def line_inward(value, wire):
    n = lax.axis_size("col")
    got = jnp.zeros_like(value).astype(wire)
    for s in range(n // 2 - 1):
        if s:
            value = value + got.astype(value.dtype)
        got = lax.ppermute(value.astype(wire), "col", [(s, s + 1), (n - 1 - s, n - 2 - s)])
    return value, got


def line_across(value, wire):
    n = lax.axis_size("col")
    pairs = [(n // 2 - 1, n // 2), (n // 2, n // 2 - 1)]
    return (value + lax.ppermute(value.astype(wire), "col", pairs).astype(value.dtype)).astype(wire)


def line_outward(value):
    n = lax.axis_size("col")
    z = lax.axis_index("col")
    for s in reversed(range(n // 2 - 1)):
        pairs = [(s + 1, s), (n - 2 - s, n - 1 - s)]
        got = lax.ppermute(value, "col", pairs)
        value = jnp.where((z == s) | (z == n - 1 - s), got, value)
    return value


def col_sum(value):
    n = lax.axis_size("col")
    for bit in range(n.bit_length() - 1):
        value = value + lax.ppermute(value, "col", [(i, i ^ (1 << bit)) for i in range(n)])
    return value


def halving(bits):
    size = 2**bits
    me = lax.axis_index("row")
    odd = me & 1
    for step in range(bits):
        even_bit = step
        odd_bit = 0 if step == 0 else bits - step
        pairs = [(i, i ^ (1 << (odd_bit if i & 1 else even_bit))) for i in range(size)]
        own = jnp.where(odd == 1, (me >> odd_bit) & 1, (me >> even_bit) & 1)
        yield pairs, own


def row_step(value, step, wire):
    bits = lax.axis_size("row").bit_length() - 1
    pairs, own = list(halving(bits))[step]
    half = value.shape[0] // 2
    give = lax.dynamic_slice_in_dim(value, (1 - own) * half, half, 0).astype(wire)
    keep = lax.dynamic_slice_in_dim(value, own * half, half, 0)
    return keep + lax.ppermute(give, "row", pairs).astype(value.dtype)


def row_gather(part):
    bits = lax.axis_size("row").bit_length() - 1
    steps = list(halving(bits))
    for pairs, own in reversed(steps):
        got = lax.ppermute(part, "row", pairs)
        low = jnp.where(own == 0, part, got)
        high = jnp.where(own == 0, got, part)
        part = jnp.concatenate([low, high], 0)
    return part


def gram_sum(gram):
    for step in range(lax.axis_size("row").bit_length() - 1):
        gram = row_step(gram, step, jnp.float32)
    return row_gather(col_sum(gram))


def share_order(k):
    n = lax.axis_size("col")
    z = lax.axis_index("col")
    low = jnp.where(k < n - 1 - z, n - 1 - k, k - (n - 1 - z))
    high = jnp.where(k < z, k, n - 1 - (k - z))
    return jnp.where(k == n - 1, z, jnp.where(z < n // 2, low, high))


def line_scatter(parts):
    n = lax.axis_size("col")
    z = lax.axis_index("col")

    def pick(t, lag):
        value = parts[t - 1]
        for d in range(1, min(n // 2, t)):
            value = jnp.where(lag == d, parts[t - 1 - d], value)
        return value

    right = left = None
    for t in range(1, n):
        up = pick(t, jnp.where(z < n // 2, z, 0))
        down = pick(t, jnp.where(z < n // 2, 0, n - 1 - z))
        if right is not None:
            up = up + right.astype(up.dtype)
            down = down + left.astype(down.dtype)
        wire = jnp.float32 if t == n - 1 else jnp.bfloat16
        right = lax.ppermute(up.astype(wire), "col", [(i, i + 1) for i in range(t)])
        left = lax.ppermute(down.astype(wire), "col", [(n - 1 - i, n - 2 - i) for i in range(t)])
        right, left = lax.optimization_barrier((right, left))
    return parts[n - 1] + right.astype(jnp.float32) + left.astype(jnp.float32)


def local(tiles, col_index, counts, sketch):
    tile_rows, slots, tile = tiles.shape[:3]
    n_col = lax.axis_size("col")
    total_rows = tile_rows * tile * lax.axis_size("row")
    counts = counts.reshape(-1)
    z = lax.axis_index("col")

    chunk = tile_rows // n_col
    halves, crossed, sent = [], [], []
    for j in range(n_col):
        live = counts
        if j == 2:
            live, halves[0] = lax.optimization_barrier((counts, halves[0]))
        elif j > 2:
            live, crossed[j - 3] = lax.optimization_barrier((counts, crossed[j - 3]))
        part = forward(tiles, col_index, live, sketch, j * chunk, chunk)
        if j >= 1:
            value, got = sent[j - 1]
            value, part = lax.optimization_barrier((value, part))
            halves.append(value + got.astype(value.dtype))
            if j >= 2:
                crossed.append(line_across(halves[j - 2], jnp.bfloat16))
        sent.append(line_inward(part, jnp.bfloat16))
    value, got = sent[-1]
    halves.append(value + got.astype(value.dtype))
    for half in halves[len(crossed):]:
        crossed.append(line_across(half, jnp.bfloat16))
    sums = [line_outward(value) for value in crossed]
    middle = n_col // 2
    back = backward(tiles, col_index, counts, sums[:middle], sketch.shape[0], 0, None)
    sums[-1], back = lax.optimization_barrier((sums[-1], back))
    first = jnp.concatenate(sums, 0)

    share = first.shape[0] // n_col
    mine = lax.dynamic_slice_in_dim(first, z * share, share, 0)
    gram = lax.dot_general(mine, mine, TN, preferred_element_type=jnp.float32)
    wires = (jnp.float32, jnp.bfloat16, jnp.float32)
    bits = lax.axis_size("row").bit_length() - 1
    for j in range(middle, n_col):
        live, gram = lax.optimization_barrier((counts, gram))
        back = backward(tiles, col_index, live, sums[j:j + 1], sketch.shape[0], j * chunk, back)
        if j - middle < bits:
            gram = row_step(gram, j - middle, jnp.float32)
        gram, back = lax.optimization_barrier((gram, back))
    part = row_step(back, 0, wires[0])
    for k in range(min(n_col - middle, bits), bits):
        gram = row_step(gram, k, jnp.float32)
    gram = col_sum(gram)
    gram, part = lax.optimization_barrier((gram, part))
    if bits > 1:
        part = row_step(part, 1, wires[1])
    gram = row_gather(gram)
    gram, part = lax.optimization_barrier((gram, part))
    for k in range(2, bits):
        part = row_step(part, k, wires[2])
    unused, inverse = cholesky(gram, 1.0 / total_rows)
    part = lax.dot_general(part, inverse, NT, precision=HI, preferred_element_type=jnp.float32)
    back = row_gather(part.astype(jnp.bfloat16))

    parts = [
        forward(tiles, col_index, counts, back, share_order(k) * chunk, chunk) for k in range(n_col)
    ]
    second = line_scatter(parts)
    gram = lax.dot_general(second, second, TN, precision=HI, preferred_element_type=jnp.float32)
    factor, inverse = cholesky(gram_sum(gram), 1.0 / total_rows)
    basis = lax.dot_general(second, inverse, NT, precision=HI, preferred_element_type=jnp.float32)
    return (basis, factor)


def solution(mesh):
    return jax.shard_map(
        local,
        mesh=mesh,
        in_specs=(P("row", "col", None, None), P("row", "col"), P("row", "col"), P("col", None)),
        out_specs=(P(("row", "col"), None), P()),
        check_vma=False,
    )
```

```python
import functools

import jax
import jax.numpy as jnp
from jax import lax
from jax.experimental import pallas as pl
from jax.experimental.pallas import tpu as pltpu
from jax.sharding import PartitionSpec as P

HI = lax.Precision.HIGHEST
NT = (((1,), (1,)), ((), ()))
TN = (((0,), (0,)), ((), ()))


def forward_body(group, base_ref, idx_ref, cnt_ref, t_ref, x_ref, o_ref, h_ref, acc_ref):
    tile = t_ref.shape[2]
    row = pl.program_id(0) + base_ref[0]
    count = cnt_ref[row]
    acc_ref[...] = jnp.zeros_like(acc_ref)

    def step(p, carry):
        lhs, rhs = [], []
        for q in range(group):
            s = p * group + q
            t = t_ref[0, s]
            lhs.append(t if q == 0 else jnp.where(s < count, t, jnp.zeros_like(t)))
            c = pl.multiple_of(idx_ref[row, s] * tile, tile)
            rhs.append(x_ref[pl.ds(c, tile), :])
        acc_ref[...] += jnp.dot(
            jnp.concatenate(lhs, 1), jnp.concatenate(rhs, 0), preferred_element_type=jnp.float32
        )
        return carry

    lax.fori_loop(0, (count + group - 1) // group, step, 0)
    o_ref[...] = acc_ref[...]
    h_ref[...] = acc_ref[...].astype(h_ref.dtype)


def forward(tiles, col_index, counts, x, base, rows):
    slots, tile = tiles.shape[1], tiles.shape[2]
    width = x.shape[1]
    group = next(g for g in (8, 4, 2, 1) if slots % g == 0)
    return pl.pallas_call(
        functools.partial(forward_body, group),
        out_shape=[
            jax.ShapeDtypeStruct((rows * tile, width), jnp.float32),
            jax.ShapeDtypeStruct((rows * tile, width), jnp.bfloat16),
        ],
        grid_spec=pltpu.PrefetchScalarGridSpec(
            num_scalar_prefetch=3,
            grid=(rows,),
            in_specs=[
                pl.BlockSpec((1, slots, tile, tile), lambda r, at, *_: (r + at[0], 0, 0, 0)),
                pl.BlockSpec(memory_space=pltpu.VMEM),
            ],
            out_specs=[pl.BlockSpec((tile, width), lambda r, *_: (r, 0))] * 2,
            scratch_shapes=[pltpu.VMEM((tile, width), jnp.float32)],
        ),
        name="forward_rows",
    )(jnp.full((1,), base, jnp.int32), col_index, counts, tiles, x)


def backward_body(group, base, panels, idx_ref, cnt_ref, t_ref, *refs):
    z_ref = refs[-1]
    tile = t_ref.shape[2]
    at = pl.program_id(0)
    each = pl.num_programs(0) // panels
    row = at + base
    count = cnt_ref[row]
    f = refs[0][...]
    for k in range(1, panels):
        f = jnp.where(at >= k * each, refs[k][...], f)

    @pl.when(at == 0)
    def _():
        z_ref[...] = refs[panels][...] if len(refs) > panels + 1 else jnp.zeros_like(z_ref)

    def step(p, carry):
        lhs = []
        for q in range(group):
            s = p * group + q
            t = t_ref[0, s]
            lhs.append(t if q == 0 else jnp.where(s < count, t, jnp.zeros_like(t)))
        out = lax.dot_general(
            jnp.concatenate(lhs, 1), f, TN, preferred_element_type=jnp.float32
        )
        for q in range(group):
            c = pl.multiple_of(idx_ref[row, p * group + q] * tile, tile)
            z_ref[pl.ds(c, tile), :] += out[q * tile:(q + 1) * tile]
        return carry

    lax.fori_loop(0, (count + group - 1) // group, step, 0)


def backward(tiles, col_index, counts, panels, col_rows, base, total):
    slots, tile = tiles.shape[1], tiles.shape[2]
    width = panels[0].shape[1]
    each = panels[0].shape[0] // tile
    group = next(g for g in (4, 2, 1) if slots % g == 0)
    whole = pl.BlockSpec(memory_space=pltpu.VMEM)
    more = () if total is None else (total,)

    def panel_map(k):
        return lambda r, *_: (jnp.clip(r - k * each, 0, each - 1), 0)

    return pl.pallas_call(
        functools.partial(backward_body, group, base, len(panels)),
        out_shape=jax.ShapeDtypeStruct((col_rows, width), jnp.float32),
        grid_spec=pltpu.PrefetchScalarGridSpec(
            num_scalar_prefetch=2,
            grid=(each * len(panels),),
            in_specs=[pl.BlockSpec((1, slots, tile, tile), lambda r, *_: (r + base, 0, 0, 0))]
            + [pl.BlockSpec((tile, width), panel_map(k)) for k in range(len(panels))]
            + [whole] * len(more),
            out_specs=whole,
        ),
        name="backward_rows",
    )(col_index, counts, tiles, *panels, *more)


def factor_block(read, r_ref, t_ref, group):
    n = 128
    vr = n // 8
    a = [read(v) for v in range(vr)]
    lane = lax.broadcasted_iota(jnp.int32, (8, n), 1)
    sub = lax.broadcasted_iota(jnp.int32, (8, n), 0)
    e = [(lane == sub + 8 * v).astype(jnp.float32) for v in range(vr)]
    full = lambda x: jnp.broadcast_to(x, (8, n))
    for g in range(n // group):
        j0 = g * group
        v0, o = j0 // 8, j0 % 8
        P = [full(a[v0][o + k:o + k + 1, :]) for k in range(group)]
        PE = [full(e[v0][o + k:o + k + 1, :]) for k in range(group)]
        el = [[full(P[i][:, j0 + k:j0 + k + 1]) for k in range(i + 1)] for i in range(group)]
        vs = [v for v in range(vr) if v > v0 or (v == v0 and o + group < 8)]
        mult = {v: [full(a[v][:, j0 + k:j0 + k + 1]) for k in range(group)] for v in vs}
        R, RE, S = [], [], []
        W = [None] * group
        WE = [None] * group
        L = [[None] * group for _ in range(group)]
        for c in range(group):
            inv = lax.rsqrt(el[c][c])
            for i in range(c + 1, group):
                L[i][c] = el[i][c] * inv
            for i in range(c + 1, group):
                for k in range(c + 1, i + 1):
                    el[i][k] = el[i][k] - L[i][c] * L[k][c]
            s = []
            for k in range(c):
                t = L[c][k] * S[k][k]
                for j in range(k + 1, c):
                    t = t + L[c][j] * S[j][k]
                s.append(-(t * inv))
            s.append(inv)
            S.append(s)
            r = P[c] * s[c]
            re = PE[c] * s[c]
            for k in range(c):
                r = r + P[k] * s[k]
                re = re + PE[k] * s[k]
            R.append(r); RE.append(re)
            for k in range(c + 1):
                W[k] = s[k] * r if W[k] is None else W[k] + s[k] * r
                WE[k] = s[k] * re if WE[k] is None else WE[k] + s[k] * re
            r_ref[j0 + c:j0 + c + 1, :] = r[0:1, :]
            t_ref[j0 + c:j0 + c + 1, :] = re[0:1, :]
        for v in vs:
            u = mult[v][0] * W[0]
            ue = mult[v][0] * WE[0]
            for k in range(1, group):
                u = u + mult[v][k] * W[k]
                ue = ue + mult[v][k] * WE[k]
            a[v] = a[v] - u
            e[v] = e[v] - ue


def chol_body(scale, group, g_ref, r_ref, t_ref, w_ref, rk_ref, tk_ref):
    n = g_ref.shape[0]
    b = 128
    w_ref[...] = g_ref[...] * scale

    def block(k, carry):
        at = pl.multiple_of(k * b, b)

        def read(v):
            return w_ref[pl.ds(pl.multiple_of(at + 8 * v, 8), 8), pl.ds(at, b)]

        factor_block(read, rk_ref, tk_ref, group)
        inv = tk_ref[...]
        x = jnp.dot(inv, w_ref[pl.ds(at, b), :], precision=HI, preferred_element_type=jnp.float32)
        row = lax.broadcasted_iota(jnp.int32, x.shape, 0) + at
        col = lax.broadcasted_iota(jnp.int32, x.shape, 1)
        r_ref[pl.ds(at, b), :] = jnp.where(col >= at + b, x, 0.0)
        r_ref[pl.ds(at, b), pl.ds(at, b)] = jnp.where(
            col[:, :b] >= row[:, :b] - at, rk_ref[...], 0.0
        )
        inv = jnp.where(col[:, :b] <= row[:, :b] - at, inv, 0.0)
        t_ref[pl.ds(at, b), :] = jnp.where(col < at, x, 0.0)
        t_ref[pl.ds(at, b), pl.ds(at, b)] = inv
        w_ref[pl.ds(at, b), :] = x
        w_ref[pl.ds(at, b), pl.ds(at, b)] = inv

        def below(i, carry):
            to = pl.multiple_of(i * b, b)
            l = r_ref[pl.ds(at, b), pl.ds(to, b)]
            w_ref[pl.ds(to, b), pl.ds(at, b)] = jnp.zeros((b, b), jnp.float32)
            w_ref[pl.ds(to, b), :] -= lax.dot_general(
                l, w_ref[pl.ds(at, b), :], TN, precision=HI, preferred_element_type=jnp.float32
            )
            return carry

        lax.fori_loop(k + 1, n // b, below, 0)
        return carry

    lax.fori_loop(0, n // b, block, 0)


def cholesky(gram, scale, group=8):
    n = gram.shape[0]
    s = jax.ShapeDtypeStruct((n, n), jnp.float32)
    return pl.pallas_call(
        functools.partial(chol_body, scale, group),
        out_shape=(s, s),
        scratch_shapes=[
            pltpu.VMEM((n, n), jnp.float32),
            pltpu.VMEM((128, 128), jnp.float32),
            pltpu.VMEM((128, 128), jnp.float32),
        ],
        name="factorize",
    )(gram)


def line_inward(value, rounded):
    n = lax.axis_size("col")
    got = jnp.zeros_like(rounded)
    for s in range(n // 2 - 1):
        if s:
            value = value + got.astype(value.dtype)
            rounded = value.astype(rounded.dtype)
        got = lax.ppermute(rounded, "col", [(s, s + 1), (n - 1 - s, n - 2 - s)])
    return value, got


def line_across(value, wire):
    n = lax.axis_size("col")
    pairs = [(n // 2 - 1, n // 2), (n // 2, n // 2 - 1)]
    return (value + lax.ppermute(value.astype(wire), "col", pairs).astype(value.dtype)).astype(wire)


def line_outward(value):
    n = lax.axis_size("col")
    z = lax.axis_index("col")
    for s in reversed(range(n // 2 - 1)):
        pairs = [(s + 1, s), (n - 2 - s, n - 1 - s)]
        got = lax.ppermute(value, "col", pairs)
        value = jnp.where((z == s) | (z == n - 1 - s), got, value)
    return value


def col_sum(value):
    n = lax.axis_size("col")
    for bit in range(n.bit_length() - 1):
        value = value + lax.ppermute(value, "col", [(i, i ^ (1 << bit)) for i in range(n)])
    return value


def halving(bits):
    size = 2**bits
    me = lax.axis_index("row")
    odd = me & 1
    for step in range(bits):
        even_bit = step
        odd_bit = 0 if step == 0 else bits - step
        pairs = [(i, i ^ (1 << (odd_bit if i & 1 else even_bit))) for i in range(size)]
        own = jnp.where(odd == 1, (me >> odd_bit) & 1, (me >> even_bit) & 1)
        yield pairs, own


def row_step(value, step, wire):
    bits = lax.axis_size("row").bit_length() - 1
    pairs, own = list(halving(bits))[step]
    half = value.shape[0] // 2
    give = lax.dynamic_slice_in_dim(value, (1 - own) * half, half, 0).astype(wire)
    keep = lax.dynamic_slice_in_dim(value, own * half, half, 0)
    return keep + lax.ppermute(give, "row", pairs).astype(value.dtype)


def row_gather(part):
    bits = lax.axis_size("row").bit_length() - 1
    steps = list(halving(bits))
    for pairs, own in reversed(steps):
        got = lax.ppermute(part, "row", pairs)
        low = jnp.where(own == 0, part, got)
        high = jnp.where(own == 0, got, part)
        part = jnp.concatenate([low, high], 0)
    return part


def gram_sum(gram):
    for step in range(lax.axis_size("row").bit_length() - 1):
        gram = row_step(gram, step, jnp.float32)
    return row_gather(col_sum(gram))


def share_order(k):
    n = lax.axis_size("col")
    z = lax.axis_index("col")
    low = jnp.where(k < n - 1 - z, n - 1 - k, k - (n - 1 - z))
    high = jnp.where(k < z, k, n - 1 - (k - z))
    return jnp.where(k == n - 1, z, jnp.where(z < n // 2, low, high))


def line_scatter(parts, rounded):
    n = lax.axis_size("col")
    z = lax.axis_index("col")

    def pick(t, lag):
        value = parts[t - 1]
        for d in range(1, min(n // 2, t)):
            value = jnp.where(lag == d, parts[t - 1 - d], value)
        return value

    right = left = None
    for t in range(1, n):
        if t == 1:
            up = down = rounded
        else:
            up = pick(t, jnp.where(z < n // 2, z, 0))
            down = pick(t, jnp.where(z < n // 2, 0, n - 1 - z))
            up = up + right.astype(up.dtype)
            down = down + left.astype(down.dtype)
        wire = jnp.float32 if t == n - 1 else jnp.bfloat16
        right = lax.ppermute(up.astype(wire), "col", [(i, i + 1) for i in range(t)])
        left = lax.ppermute(down.astype(wire), "col", [(n - 1 - i, n - 2 - i) for i in range(t)])
        right, left = lax.optimization_barrier((right, left))
    return parts[n - 1] + right.astype(jnp.float32) + left.astype(jnp.float32)


def local(tiles, col_index, counts, sketch):
    tile_rows, slots, tile = tiles.shape[:3]
    n_col = lax.axis_size("col")
    total_rows = tile_rows * tile * lax.axis_size("row")
    counts = counts.reshape(-1)
    z = lax.axis_index("col")

    chunk = tile_rows // n_col
    near = pltpu.with_memory_space_constraint(sketch, pltpu.VMEM)
    halves, crossed, sent = [], [], []
    for j in range(n_col):
        live = counts
        if j == 2:
            live, halves[0] = lax.optimization_barrier((counts, halves[0]))
        elif j > 2:
            live, crossed[j - 3] = lax.optimization_barrier((counts, crossed[j - 3]))
        part, rounded = forward(tiles, col_index, live, near, j * chunk, chunk)
        if j >= 1:
            value, got = sent[j - 1]
            value, part = lax.optimization_barrier((value, part))
            halves.append(value + got.astype(value.dtype))
            if j >= 2:
                crossed.append(line_across(halves[j - 2], jnp.bfloat16))
        sent.append(line_inward(part, rounded))
    value, got = sent[-1]
    halves.append(value + got.astype(value.dtype))
    for half in halves[len(crossed):]:
        crossed.append(line_across(half, jnp.bfloat16))
    sums = [line_outward(value) for value in crossed]
    middle = n_col // 2
    back = backward(tiles, col_index, counts, sums[:middle], sketch.shape[0], 0, None)
    sums[-1], back = lax.optimization_barrier((sums[-1], back))
    first = jnp.concatenate(sums, 0)

    share = first.shape[0] // n_col
    mine = lax.dynamic_slice_in_dim(first, z * share, share, 0)
    gram = lax.dot_general(mine, mine, TN, preferred_element_type=jnp.float32)
    wires = (jnp.float32, jnp.bfloat16, jnp.float32)
    bits = lax.axis_size("row").bit_length() - 1
    for j in range(middle, n_col):
        live, gram = lax.optimization_barrier((counts, gram))
        back = backward(tiles, col_index, live, sums[j:j + 1], sketch.shape[0], j * chunk, back)
        if j - middle < bits:
            gram = row_step(gram, j - middle, jnp.float32)
        gram, back = lax.optimization_barrier((gram, back))
    part = row_step(back, 0, wires[0])
    for k in range(min(n_col - middle, bits), bits):
        gram = row_step(gram, k, jnp.float32)
    gram = col_sum(gram)
    gram, part = lax.optimization_barrier((gram, part))
    if bits > 1:
        part = row_step(part, 1, wires[1])
    gram = row_gather(gram)
    gram, part = lax.optimization_barrier((gram, part))
    for k in range(2, bits):
        part = row_step(part, k, wires[2])
    unused, inverse = cholesky(gram, 1.0 / total_rows)
    part = lax.dot_general(part, inverse, NT, precision=HI, preferred_element_type=jnp.float32)
    back = row_gather(part.astype(jnp.bfloat16))
    back = pltpu.with_memory_space_constraint(back, pltpu.VMEM)

    parts = [
        forward(tiles, col_index, counts, back, share_order(k) * chunk, chunk) for k in range(n_col)
    ]
    second = line_scatter([part for part, _ in parts], parts[0][1])
    gram = lax.dot_general(second, second, TN, precision=HI, preferred_element_type=jnp.float32)
    factor, inverse = cholesky(gram_sum(gram), 1.0 / total_rows)
    basis = lax.dot_general(second, inverse, NT, precision=HI, preferred_element_type=jnp.float32)
    return (basis, factor)


def solution(mesh):
    return jax.shard_map(
        local,
        mesh=mesh,
        in_specs=(P("row", "col", None, None), P("row", "col"), P("row", "col"), P("col", None)),
        out_specs=(P(("row", "col"), None), P()),
        check_vma=False,
    )
```

```python
import functools

import jax
import jax.numpy as jnp
from jax import lax
from jax.experimental import pallas as pl
from jax.experimental.pallas import tpu as pltpu
from jax.sharding import PartitionSpec as P

HI = lax.Precision.HIGHEST
NT = (((1,), (1,)), ((), ()))
TN = (((0,), (0,)), ((), ()))


def forward_body(group, base, meta_ref, t_ref, x_ref, o_ref, h_ref, acc_ref):
    slots, tile = t_ref.shape[1], t_ref.shape[2]
    row = pl.program_id(0) + (meta_ref[0, slots + 1] if base is None else base)
    count = meta_ref[row, slots]
    acc_ref[...] = jnp.zeros_like(acc_ref)

    def step(p, carry):
        lhs, rhs = [], []
        for q in range(group):
            s = p * group + q
            t = t_ref[0, s]
            lhs.append(t if q == 0 else jnp.where(s < count, t, jnp.zeros_like(t)))
            c = pl.multiple_of(meta_ref[row, s] * tile, tile)
            rhs.append(x_ref[pl.ds(c, tile), :])
        acc_ref[...] += jnp.dot(
            jnp.concatenate(lhs, 1), jnp.concatenate(rhs, 0), preferred_element_type=jnp.float32
        )
        return carry

    lax.fori_loop(0, (count + group - 1) // group, step, 0)
    o_ref[...] = acc_ref[...]
    h_ref[...] = acc_ref[...].astype(h_ref.dtype)


def forward(tiles, meta, x, base, rows):
    slots, tile = tiles.shape[1], tiles.shape[2]
    width = x.shape[1]
    group = next(g for g in (8, 4, 2, 1) if slots % g == 0)

    def tile_map(r, meta_ref):
        return (r + (meta_ref[0, slots + 1] if base is None else base), 0, 0, 0)

    return pl.pallas_call(
        functools.partial(forward_body, group, base),
        out_shape=[
            jax.ShapeDtypeStruct((rows * tile, width), jnp.float32),
            jax.ShapeDtypeStruct((rows * tile, width), jnp.bfloat16),
        ],
        grid_spec=pltpu.PrefetchScalarGridSpec(
            num_scalar_prefetch=1,
            grid=(rows,),
            in_specs=[
                pl.BlockSpec((1, slots, tile, tile), tile_map),
                pl.BlockSpec(memory_space=pltpu.VMEM),
            ],
            out_specs=[pl.BlockSpec((tile, width), lambda r, *_: (r, 0))] * 2,
            scratch_shapes=[pltpu.VMEM((tile, width), jnp.float32)],
        ),
        name="forward_rows",
    )(meta, tiles, x)


def backward_body(group, base, panels, meta_ref, t_ref, *refs):
    z_ref = refs[-1]
    slots, tile = t_ref.shape[1], t_ref.shape[2]
    at = pl.program_id(0)
    each = pl.num_programs(0) // panels
    row = at + base
    count = meta_ref[row, slots]
    f = refs[0][...]
    for k in range(1, panels):
        f = jnp.where(at >= k * each, refs[k][...], f)

    @pl.when(at == 0)
    def _():
        z_ref[...] = refs[panels][...] if len(refs) > panels + 1 else jnp.zeros_like(z_ref)

    def step(p, carry):
        lhs = []
        for q in range(group):
            s = p * group + q
            t = t_ref[0, s]
            lhs.append(t if q == 0 else jnp.where(s < count, t, jnp.zeros_like(t)))
        out = lax.dot_general(
            jnp.concatenate(lhs, 1), f, TN, preferred_element_type=jnp.float32
        )
        for q in range(group):
            c = pl.multiple_of(meta_ref[row, p * group + q] * tile, tile)
            z_ref[pl.ds(c, tile), :] += out[q * tile:(q + 1) * tile]
        return carry

    lax.fori_loop(0, (count + group - 1) // group, step, 0)


def backward(tiles, meta, panels, col_rows, base, total):
    slots, tile = tiles.shape[1], tiles.shape[2]
    width = panels[0].shape[1]
    each = panels[0].shape[0] // tile
    group = next(g for g in (4, 2, 1) if slots % g == 0)
    whole = pl.BlockSpec(memory_space=pltpu.VMEM)
    more = () if total is None else (total,)

    def panel_map(k):
        return lambda r, *_: (jnp.clip(r - k * each, 0, each - 1), 0)

    return pl.pallas_call(
        functools.partial(backward_body, group, base, len(panels)),
        out_shape=jax.ShapeDtypeStruct((col_rows, width), jnp.float32),
        grid_spec=pltpu.PrefetchScalarGridSpec(
            num_scalar_prefetch=1,
            grid=(each * len(panels),),
            in_specs=[pl.BlockSpec((1, slots, tile, tile), lambda r, *_: (r + base, 0, 0, 0))]
            + [pl.BlockSpec((tile, width), panel_map(k)) for k in range(len(panels))]
            + [whole] * len(more),
            out_specs=whole,
        ),
        name="backward_rows",
    )(meta, tiles, *panels, *more)


def factor_block(read, r_ref, t_ref, group):
    n = 128
    vr = n // 8
    a = [read(v) for v in range(vr)]
    lane = lax.broadcasted_iota(jnp.int32, (8, n), 1)
    sub = lax.broadcasted_iota(jnp.int32, (8, n), 0)
    e = [(lane == sub + 8 * v).astype(jnp.float32) for v in range(vr)]
    full = lambda x: jnp.broadcast_to(x, (8, n))
    for g in range(n // group):
        j0 = g * group
        v0, o = j0 // 8, j0 % 8
        P = [full(a[v0][o + k:o + k + 1, :]) for k in range(group)]
        PE = [full(e[v0][o + k:o + k + 1, :]) for k in range(group)]
        el = [[full(P[i][:, j0 + k:j0 + k + 1]) for k in range(i + 1)] for i in range(group)]
        vs = [v for v in range(vr) if v > v0 or (v == v0 and o + group < 8)]
        mult = {v: [full(a[v][:, j0 + k:j0 + k + 1]) for k in range(group)] for v in vs}
        R, RE, S = [], [], []
        W = [None] * group
        WE = [None] * group
        L = [[None] * group for _ in range(group)]
        for c in range(group):
            inv = lax.rsqrt(el[c][c])
            for i in range(c + 1, group):
                L[i][c] = el[i][c] * inv
            for i in range(c + 1, group):
                for k in range(c + 1, i + 1):
                    el[i][k] = el[i][k] - L[i][c] * L[k][c]
            s = []
            for k in range(c):
                t = L[c][k] * S[k][k]
                for j in range(k + 1, c):
                    t = t + L[c][j] * S[j][k]
                s.append(-(t * inv))
            s.append(inv)
            S.append(s)
            r = P[c] * s[c]
            re = PE[c] * s[c]
            for k in range(c):
                r = r + P[k] * s[k]
                re = re + PE[k] * s[k]
            R.append(r); RE.append(re)
            for k in range(c + 1):
                W[k] = s[k] * r if W[k] is None else W[k] + s[k] * r
                WE[k] = s[k] * re if WE[k] is None else WE[k] + s[k] * re
            r_ref[j0 + c:j0 + c + 1, :] = r[0:1, :]
            t_ref[j0 + c:j0 + c + 1, :] = re[0:1, :]
        for v in vs:
            u = mult[v][0] * W[0]
            ue = mult[v][0] * WE[0]
            for k in range(1, group):
                u = u + mult[v][k] * W[k]
                ue = ue + mult[v][k] * WE[k]
            a[v] = a[v] - u
            e[v] = e[v] - ue


def chol_body(scale, group, g_ref, r_ref, t_ref, w_ref, rk_ref, tk_ref):
    n = g_ref.shape[0]
    b = 128
    w_ref[...] = g_ref[...] * scale

    def block(k, carry):
        at = pl.multiple_of(k * b, b)

        def read(v):
            return w_ref[pl.ds(pl.multiple_of(at + 8 * v, 8), 8), pl.ds(at, b)]

        factor_block(read, rk_ref, tk_ref, group)
        inv = tk_ref[...]
        x = jnp.dot(inv, w_ref[pl.ds(at, b), :], precision=HI, preferred_element_type=jnp.float32)
        row = lax.broadcasted_iota(jnp.int32, x.shape, 0) + at
        col = lax.broadcasted_iota(jnp.int32, x.shape, 1)
        r_ref[pl.ds(at, b), :] = jnp.where(col >= at + b, x, 0.0)
        r_ref[pl.ds(at, b), pl.ds(at, b)] = jnp.where(
            col[:, :b] >= row[:, :b] - at, rk_ref[...], 0.0
        )
        inv = jnp.where(col[:, :b] <= row[:, :b] - at, inv, 0.0)
        t_ref[pl.ds(at, b), :] = jnp.where(col < at, x, 0.0)
        t_ref[pl.ds(at, b), pl.ds(at, b)] = inv
        w_ref[pl.ds(at, b), :] = x
        w_ref[pl.ds(at, b), pl.ds(at, b)] = inv

        def below(i, carry):
            to = pl.multiple_of(i * b, b)
            l = r_ref[pl.ds(at, b), pl.ds(to, b)]
            w_ref[pl.ds(to, b), pl.ds(at, b)] = jnp.zeros((b, b), jnp.float32)
            w_ref[pl.ds(to, b), :] -= lax.dot_general(
                l, w_ref[pl.ds(at, b), :], TN, precision=HI, preferred_element_type=jnp.float32
            )
            return carry

        lax.fori_loop(k + 1, n // b, below, 0)
        return carry

    lax.fori_loop(0, n // b, block, 0)


def cholesky(gram, scale, group=8):
    n = gram.shape[0]
    s = jax.ShapeDtypeStruct((n, n), jnp.float32)
    return pl.pallas_call(
        functools.partial(chol_body, scale, group),
        out_shape=(s, s),
        scratch_shapes=[
            pltpu.VMEM((n, n), jnp.float32),
            pltpu.VMEM((128, 128), jnp.float32),
            pltpu.VMEM((128, 128), jnp.float32),
        ],
        name="factorize",
    )(gram)


def line_inward(value, rounded):
    n = lax.axis_size("col")
    got = jnp.zeros_like(rounded)
    for s in range(n // 2 - 1):
        if s:
            value = value + got.astype(value.dtype)
            rounded = value.astype(rounded.dtype)
        got = lax.ppermute(rounded, "col", [(s, s + 1), (n - 1 - s, n - 2 - s)])
    return value, got


def line_across(value, wire):
    n = lax.axis_size("col")
    pairs = [(n // 2 - 1, n // 2), (n // 2, n // 2 - 1)]
    return (value + lax.ppermute(value.astype(wire), "col", pairs).astype(value.dtype)).astype(wire)


def line_outward(value):
    n = lax.axis_size("col")
    z = lax.axis_index("col")
    for s in reversed(range(n // 2 - 1)):
        pairs = [(s + 1, s), (n - 2 - s, n - 1 - s)]
        got = lax.ppermute(value, "col", pairs)
        value = jnp.where((z == s) | (z == n - 1 - s), got, value)
    return value


def col_sum(value):
    n = lax.axis_size("col")
    for bit in range(n.bit_length() - 1):
        value = value + lax.ppermute(value, "col", [(i, i ^ (1 << bit)) for i in range(n)])
    return value


def halving(bits):
    size = 2**bits
    me = lax.axis_index("row")
    odd = me & 1
    for step in range(bits):
        even_bit = step
        odd_bit = 0 if step == 0 else bits - step
        pairs = [(i, i ^ (1 << (odd_bit if i & 1 else even_bit))) for i in range(size)]
        own = jnp.where(odd == 1, (me >> odd_bit) & 1, (me >> even_bit) & 1)
        yield pairs, own


def row_step(value, step, wire):
    bits = lax.axis_size("row").bit_length() - 1
    pairs, own = list(halving(bits))[step]
    half = value.shape[0] // 2
    give = lax.dynamic_slice_in_dim(value, (1 - own) * half, half, 0).astype(wire)
    keep = lax.dynamic_slice_in_dim(value, own * half, half, 0)
    return keep + lax.ppermute(give, "row", pairs).astype(value.dtype)


def row_gather(part):
    bits = lax.axis_size("row").bit_length() - 1
    steps = list(halving(bits))
    for pairs, own in reversed(steps):
        got = lax.ppermute(part, "row", pairs)
        low = jnp.where(own == 0, part, got)
        high = jnp.where(own == 0, got, part)
        part = jnp.concatenate([low, high], 0)
    return part


def gram_sum(gram):
    for step in range(lax.axis_size("row").bit_length() - 1):
        gram = row_step(gram, step, jnp.float32)
    return row_gather(col_sum(gram))


def share_order(k):
    n = lax.axis_size("col")
    z = lax.axis_index("col")
    low = jnp.where(k < n - 1 - z, n - 1 - k, k - (n - 1 - z))
    high = jnp.where(k < z, k, n - 1 - (k - z))
    return jnp.where(k == n - 1, z, jnp.where(z < n // 2, low, high))


def line_scatter(parts, rounded):
    n = lax.axis_size("col")
    z = lax.axis_index("col")

    def pick(t, lag):
        value = parts[t - 1]
        for d in range(1, min(n // 2, t)):
            value = jnp.where(lag == d, parts[t - 1 - d], value)
        return value

    right = left = None
    for t in range(1, n):
        if t == 1:
            up = down = rounded
        else:
            up = pick(t, jnp.where(z < n // 2, z, 0))
            down = pick(t, jnp.where(z < n // 2, 0, n - 1 - z))
            up = up + right.astype(up.dtype)
            down = down + left.astype(down.dtype)
        wire = jnp.float32 if t == n - 1 else jnp.bfloat16
        right = lax.ppermute(up.astype(wire), "col", [(i, i + 1) for i in range(t)])
        left = lax.ppermute(down.astype(wire), "col", [(n - 1 - i, n - 2 - i) for i in range(t)])
        right, left = lax.optimization_barrier((right, left))
    return parts[n - 1] + right.astype(jnp.float32) + left.astype(jnp.float32)


def local(tiles, col_index, counts, sketch):
    tile_rows, slots, tile = tiles.shape[:3]
    n_col = lax.axis_size("col")
    total_rows = tile_rows * tile * lax.axis_size("row")
    z = lax.axis_index("col")

    def table(base):
        start = jnp.broadcast_to(base, (tile_rows, 1)).astype(jnp.int32)
        return jnp.concatenate([col_index, counts.reshape(-1, 1), start], 1)

    meta = table(0)

    chunk = tile_rows // n_col
    near = pltpu.with_memory_space_constraint(sketch, pltpu.VMEM)
    halves, crossed, sent = [], [], []
    for j in range(n_col):
        live = meta
        if j == 2:
            live, halves[0] = lax.optimization_barrier((meta, halves[0]))
        elif j > 2:
            live, crossed[j - 3] = lax.optimization_barrier((meta, crossed[j - 3]))
        part, rounded = forward(tiles, live, near, j * chunk, chunk)
        if j >= 1:
            value, got = sent[j - 1]
            value, part = lax.optimization_barrier((value, part))
            halves.append(value + got.astype(value.dtype))
            if j >= 2:
                crossed.append(line_across(halves[j - 2], jnp.bfloat16))
        sent.append(line_inward(part, rounded))
    value, got = sent[-1]
    halves.append(value + got.astype(value.dtype))
    for half in halves[len(crossed):]:
        crossed.append(line_across(half, jnp.bfloat16))
    sums = [line_outward(value) for value in crossed]
    middle = n_col // 2
    back = backward(tiles, meta, sums[:middle], sketch.shape[0], 0, None)
    sums[-1], back = lax.optimization_barrier((sums[-1], back))
    first = jnp.concatenate(sums, 0)

    share = first.shape[0] // n_col
    mine = lax.dynamic_slice_in_dim(first, z * share, share, 0)
    gram = lax.dot_general(mine, mine, TN, preferred_element_type=jnp.float32)
    wires = (jnp.float32, jnp.bfloat16, jnp.float32)
    bits = lax.axis_size("row").bit_length() - 1
    for j in range(middle, n_col):
        live, gram = lax.optimization_barrier((meta, gram))
        back = backward(tiles, live, sums[j:j + 1], sketch.shape[0], j * chunk, back)
        if j - middle < bits:
            gram = row_step(gram, j - middle, jnp.float32)
        gram, back = lax.optimization_barrier((gram, back))
    part = row_step(back, 0, wires[0])
    for k in range(min(n_col - middle, bits), bits):
        gram = row_step(gram, k, jnp.float32)
    gram = col_sum(gram)
    gram, part = lax.optimization_barrier((gram, part))
    if bits > 1:
        part = row_step(part, 1, wires[1])
    gram = row_gather(gram)
    gram, part = lax.optimization_barrier((gram, part))
    for k in range(2, bits):
        part = row_step(part, k, wires[2])
    unused, inverse = cholesky(gram, 1.0 / total_rows)
    part = lax.dot_general(part, inverse, NT, precision=HI, preferred_element_type=jnp.float32)
    back = row_gather(part.astype(jnp.bfloat16))
    back = pltpu.with_memory_space_constraint(back, pltpu.VMEM)

    parts = [
        forward(tiles, table(share_order(k) * chunk), back, None, chunk) for k in range(n_col)
    ]
    second = line_scatter([part for part, _ in parts], parts[0][1])
    gram = lax.dot_general(second, second, TN, precision=HI, preferred_element_type=jnp.float32)
    factor, inverse = cholesky(gram_sum(gram), 1.0 / total_rows)
    basis = lax.dot_general(second, inverse, NT, precision=HI, preferred_element_type=jnp.float32)
    return (basis, factor)


def solution(mesh):
    return jax.shard_map(
        local,
        mesh=mesh,
        in_specs=(P("row", "col", None, None), P("row", "col"), P("row", "col"), P("col", None)),
        out_specs=(P(("row", "col"), None), P()),
        check_vma=False,
    )
```

```python
import functools

import jax
import jax.numpy as jnp
from jax import lax
from jax.experimental import pallas as pl
from jax.experimental.pallas import tpu as pltpu
from jax.sharding import PartitionSpec as P

HI = lax.Precision.HIGHEST
NT = (((1,), (1,)), ((), ()))
TN = (((0,), (0,)), ((), ()))


def forward_body(group, base_ref, idx_ref, cnt_ref, t_ref, x_ref, o_ref, h_ref, acc_ref):
    tile = t_ref.shape[2]
    row = pl.program_id(0) + base_ref[0]
    count = cnt_ref[row]
    acc_ref[...] = jnp.zeros_like(acc_ref)

    def step(p, carry):
        lhs, rhs = [], []
        for q in range(group):
            s = p * group + q
            t = t_ref[0, s]
            lhs.append(t if q == 0 else jnp.where(s < count, t, jnp.zeros_like(t)))
            c = pl.multiple_of(idx_ref[row, s] * tile, tile)
            rhs.append(x_ref[pl.ds(c, tile), :])
        acc_ref[...] += jnp.dot(
            jnp.concatenate(lhs, 1), jnp.concatenate(rhs, 0), preferred_element_type=jnp.float32
        )
        return carry

    lax.fori_loop(0, (count + group - 1) // group, step, 0)
    o_ref[...] = acc_ref[...]
    h_ref[...] = acc_ref[...].astype(h_ref.dtype)


def forward(tiles, col_index, counts, x, base, rows):
    slots, tile = tiles.shape[1], tiles.shape[2]
    width = x.shape[1]
    group = next(g for g in (8, 4, 2, 1) if slots % g == 0)
    return pl.pallas_call(
        functools.partial(forward_body, group),
        out_shape=[
            jax.ShapeDtypeStruct((rows * tile, width), jnp.float32),
            jax.ShapeDtypeStruct((rows * tile, width), jnp.bfloat16),
        ],
        grid_spec=pltpu.PrefetchScalarGridSpec(
            num_scalar_prefetch=3,
            grid=(rows,),
            in_specs=[
                pl.BlockSpec((1, slots, tile, tile), lambda r, at, *_: (r + at[0], 0, 0, 0)),
                pl.BlockSpec(memory_space=pltpu.VMEM),
            ],
            out_specs=[pl.BlockSpec((tile, width), lambda r, *_: (r, 0))] * 2,
            scratch_shapes=[pltpu.VMEM((tile, width), jnp.float32)],
        ),
        name="forward_rows",
    )(jnp.full((1,), base, jnp.int32), col_index, counts, tiles, x)


def backward_body(group, base, panels, idx_ref, cnt_ref, t_ref, *refs):
    z_ref = refs[-1]
    tile = t_ref.shape[2]
    at = pl.program_id(0)
    each = pl.num_programs(0) // panels
    row = at + base
    count = cnt_ref[row]
    f = refs[0][...]
    for k in range(1, panels):
        f = jnp.where(at >= k * each, refs[k][...], f)

    @pl.when(at == 0)
    def _():
        z_ref[...] = refs[panels][...] if len(refs) > panels + 1 else jnp.zeros_like(z_ref)

    def step(p, carry):
        lhs = []
        for q in range(group):
            s = p * group + q
            t = t_ref[0, s]
            lhs.append(t if q == 0 else jnp.where(s < count, t, jnp.zeros_like(t)))
        out = lax.dot_general(
            jnp.concatenate(lhs, 1), f, TN, preferred_element_type=jnp.float32
        )
        for q in range(group):
            c = pl.multiple_of(idx_ref[row, p * group + q] * tile, tile)
            z_ref[pl.ds(c, tile), :] += out[q * tile:(q + 1) * tile]
        return carry

    lax.fori_loop(0, (count + group - 1) // group, step, 0)


def backward(tiles, col_index, counts, panels, col_rows, base, total):
    slots, tile = tiles.shape[1], tiles.shape[2]
    width = panels[0].shape[1]
    each = panels[0].shape[0] // tile
    group = next(g for g in (4, 2, 1) if slots % g == 0)
    whole = pl.BlockSpec(memory_space=pltpu.VMEM)
    more = () if total is None else (total,)

    def panel_map(k):
        return lambda r, *_: (jnp.clip(r - k * each, 0, each - 1), 0)

    return pl.pallas_call(
        functools.partial(backward_body, group, base, len(panels)),
        out_shape=jax.ShapeDtypeStruct((col_rows, width), jnp.float32),
        grid_spec=pltpu.PrefetchScalarGridSpec(
            num_scalar_prefetch=2,
            grid=(each * len(panels),),
            in_specs=[pl.BlockSpec((1, slots, tile, tile), lambda r, *_: (r + base, 0, 0, 0))]
            + [pl.BlockSpec((tile, width), panel_map(k)) for k in range(len(panels))]
            + [whole] * len(more),
            out_specs=whole,
        ),
        name="backward_rows",
    )(col_index, counts, tiles, *panels, *more)


def factor_block(read, r_ref, t_ref, group):
    n = 128
    vr = n // 8
    a = [read(v) for v in range(vr)]
    lane = lax.broadcasted_iota(jnp.int32, (8, n), 1)
    sub = lax.broadcasted_iota(jnp.int32, (8, n), 0)
    e = [(lane == sub + 8 * v).astype(jnp.float32) for v in range(vr)]
    full = lambda x: jnp.broadcast_to(x, (8, n))
    for g in range(n // group):
        j0 = g * group
        v0, o = j0 // 8, j0 % 8
        P = [full(a[v0][o + k:o + k + 1, :]) for k in range(group)]
        PE = [full(e[v0][o + k:o + k + 1, :]) for k in range(group)]
        el = [[full(P[i][:, j0 + k:j0 + k + 1]) for k in range(i + 1)] for i in range(group)]
        vs = [v for v in range(vr) if v > v0 or (v == v0 and o + group < 8)]
        mult = {v: [full(a[v][:, j0 + k:j0 + k + 1]) for k in range(group)] for v in vs}
        R, RE, S = [], [], []
        W = [None] * group
        WE = [None] * group
        L = [[None] * group for _ in range(group)]
        for c in range(group):
            inv = lax.rsqrt(el[c][c])
            for i in range(c + 1, group):
                L[i][c] = el[i][c] * inv
            for i in range(c + 1, group):
                for k in range(c + 1, i + 1):
                    el[i][k] = el[i][k] - L[i][c] * L[k][c]
            s = []
            for k in range(c):
                t = L[c][k] * S[k][k]
                for j in range(k + 1, c):
                    t = t + L[c][j] * S[j][k]
                s.append(-(t * inv))
            s.append(inv)
            S.append(s)
            r = P[c] * s[c]
            re = PE[c] * s[c]
            for k in range(c):
                r = r + P[k] * s[k]
                re = re + PE[k] * s[k]
            R.append(r); RE.append(re)
            for k in range(c + 1):
                W[k] = s[k] * r if W[k] is None else W[k] + s[k] * r
                WE[k] = s[k] * re if WE[k] is None else WE[k] + s[k] * re
            r_ref[j0 + c:j0 + c + 1, :] = r[0:1, :]
            t_ref[j0 + c:j0 + c + 1, :] = re[0:1, :]
        for v in vs:
            u = mult[v][0] * W[0]
            ue = mult[v][0] * WE[0]
            for k in range(1, group):
                u = u + mult[v][k] * W[k]
                ue = ue + mult[v][k] * WE[k]
            a[v] = a[v] - u
            e[v] = e[v] - ue


def chol_body(scale, group, g_ref, r_ref, t_ref, w_ref, rk_ref, tk_ref):
    n = g_ref.shape[0]
    b = 128
    w_ref[...] = g_ref[...] * scale

    def block(k, carry):
        at = pl.multiple_of(k * b, b)

        def read(v):
            return w_ref[pl.ds(pl.multiple_of(at + 8 * v, 8), 8), pl.ds(at, b)]

        factor_block(read, rk_ref, tk_ref, group)
        inv = tk_ref[...]
        x = jnp.dot(inv, w_ref[pl.ds(at, b), :], precision=HI, preferred_element_type=jnp.float32)
        row = lax.broadcasted_iota(jnp.int32, x.shape, 0) + at
        col = lax.broadcasted_iota(jnp.int32, x.shape, 1)
        r_ref[pl.ds(at, b), :] = jnp.where(col >= at + b, x, 0.0)
        r_ref[pl.ds(at, b), pl.ds(at, b)] = jnp.where(
            col[:, :b] >= row[:, :b] - at, rk_ref[...], 0.0
        )
        inv = jnp.where(col[:, :b] <= row[:, :b] - at, inv, 0.0)
        t_ref[pl.ds(at, b), :] = jnp.where(col < at, x, 0.0)
        t_ref[pl.ds(at, b), pl.ds(at, b)] = inv
        w_ref[pl.ds(at, b), :] = x
        w_ref[pl.ds(at, b), pl.ds(at, b)] = inv

        def below(i, carry):
            to = pl.multiple_of(i * b, b)
            l = r_ref[pl.ds(at, b), pl.ds(to, b)]
            w_ref[pl.ds(to, b), pl.ds(at, b)] = jnp.zeros((b, b), jnp.float32)
            w_ref[pl.ds(to, b), :] -= lax.dot_general(
                l, w_ref[pl.ds(at, b), :], TN, precision=HI, preferred_element_type=jnp.float32
            )
            return carry

        lax.fori_loop(k + 1, n // b, below, 0)
        return carry

    lax.fori_loop(0, n // b, block, 0)


def cholesky(gram, scale, group=8):
    n = gram.shape[0]
    s = jax.ShapeDtypeStruct((n, n), jnp.float32)
    return pl.pallas_call(
        functools.partial(chol_body, scale, group),
        out_shape=(s, s),
        scratch_shapes=[
            pltpu.VMEM((n, n), jnp.float32),
            pltpu.VMEM((128, 128), jnp.float32),
            pltpu.VMEM((128, 128), jnp.float32),
        ],
        name="factorize",
    )(gram)


def line_inward(value, rounded):
    n = lax.axis_size("col")
    got = jnp.zeros_like(rounded)
    for s in range(n // 2 - 1):
        if s:
            value = value + got.astype(value.dtype)
            rounded = value.astype(rounded.dtype)
        got = lax.ppermute(rounded, "col", [(s, s + 1), (n - 1 - s, n - 2 - s)])
    return value, got


def line_across(value, wire):
    n = lax.axis_size("col")
    pairs = [(n // 2 - 1, n // 2), (n // 2, n // 2 - 1)]
    return (value + lax.ppermute(value.astype(wire), "col", pairs).astype(value.dtype)).astype(wire)


def line_outward(value):
    n = lax.axis_size("col")
    z = lax.axis_index("col")
    for s in reversed(range(n // 2 - 1)):
        pairs = [(s + 1, s), (n - 2 - s, n - 1 - s)]
        got = lax.ppermute(value, "col", pairs)
        value = jnp.where((z == s) | (z == n - 1 - s), got, value)
    return value


def col_sum(value):
    n = lax.axis_size("col")
    for bit in range(n.bit_length() - 1):
        value = value + lax.ppermute(value, "col", [(i, i ^ (1 << bit)) for i in range(n)])
    return value


def halving(bits):
    size = 2**bits
    me = lax.axis_index("row")
    odd = me & 1
    for step in range(bits):
        even_bit = step
        odd_bit = 0 if step == 0 else bits - step
        pairs = [(i, i ^ (1 << (odd_bit if i & 1 else even_bit))) for i in range(size)]
        own = jnp.where(odd == 1, (me >> odd_bit) & 1, (me >> even_bit) & 1)
        yield pairs, own


def row_step(value, step, wire):
    bits = lax.axis_size("row").bit_length() - 1
    pairs, own = list(halving(bits))[step]
    half = value.shape[0] // 2
    give = lax.dynamic_slice_in_dim(value, (1 - own) * half, half, 0).astype(wire)
    keep = lax.dynamic_slice_in_dim(value, own * half, half, 0)
    return keep + lax.ppermute(give, "row", pairs).astype(value.dtype)


def row_gather(part):
    bits = lax.axis_size("row").bit_length() - 1
    steps = list(halving(bits))
    for pairs, own in reversed(steps):
        got = lax.ppermute(part, "row", pairs)
        mine = (jnp.arange(2) == own)[:, None, None]
        part = jnp.where(mine, part[None], got[None]).reshape(2 * part.shape[0], part.shape[1])
    return part


def gram_sum(gram):
    for step in range(lax.axis_size("row").bit_length() - 1):
        gram = row_step(gram, step, jnp.float32)
    return row_gather(col_sum(gram))


def share_order(k):
    n = lax.axis_size("col")
    z = lax.axis_index("col")
    low = jnp.where(k < n - 1 - z, n - 1 - k, k - (n - 1 - z))
    high = jnp.where(k < z, k, n - 1 - (k - z))
    return jnp.where(k == n - 1, z, jnp.where(z < n // 2, low, high))


def line_scatter(parts, rounded):
    n = lax.axis_size("col")
    z = lax.axis_index("col")

    def pick(t, lag):
        value = parts[t - 1]
        for d in range(1, min(n // 2, t)):
            value = jnp.where(lag == d, parts[t - 1 - d], value)
        return value

    right = left = None
    for t in range(1, n):
        if t == 1:
            up = down = rounded
        else:
            up = pick(t, jnp.where(z < n // 2, z, 0))
            down = pick(t, jnp.where(z < n // 2, 0, n - 1 - z))
            up = up + right.astype(up.dtype)
            down = down + left.astype(down.dtype)
        wire = jnp.float32 if t == n - 1 else jnp.bfloat16
        right = lax.ppermute(up.astype(wire), "col", [(i, i + 1) for i in range(t)])
        left = lax.ppermute(down.astype(wire), "col", [(n - 1 - i, n - 2 - i) for i in range(t)])
        right, left = lax.optimization_barrier((right, left))
    return parts[n - 1] + right.astype(jnp.float32) + left.astype(jnp.float32)


def local(tiles, col_index, counts, sketch):
    tile_rows, slots, tile = tiles.shape[:3]
    n_col = lax.axis_size("col")
    total_rows = tile_rows * tile * lax.axis_size("row")
    counts = counts.reshape(-1)
    z = lax.axis_index("col")

    chunk = tile_rows // n_col
    near = pltpu.with_memory_space_constraint(sketch, pltpu.VMEM)
    halves, crossed, sent = [], [], []
    for j in range(n_col):
        live = counts
        if j == 2:
            live, halves[0] = lax.optimization_barrier((counts, halves[0]))
        elif j > 2:
            live, crossed[j - 3] = lax.optimization_barrier((counts, crossed[j - 3]))
        part, rounded = forward(tiles, col_index, live, near, j * chunk, chunk)
        if j >= 1:
            value, got = sent[j - 1]
            value, part = lax.optimization_barrier((value, part))
            halves.append(value + got.astype(value.dtype))
            if j >= 2:
                crossed.append(line_across(halves[j - 2], jnp.bfloat16))
        sent.append(line_inward(part, rounded))
    value, got = sent[-1]
    halves.append(value + got.astype(value.dtype))
    for half in halves[len(crossed):]:
        crossed.append(line_across(half, jnp.bfloat16))
    sums = [line_outward(value) for value in crossed]
    middle = n_col // 2
    back = backward(tiles, col_index, counts, sums[:middle], sketch.shape[0], 0, None)
    sums[-1], back = lax.optimization_barrier((sums[-1], back))
    first = jnp.concatenate(sums, 0)

    share = first.shape[0] // n_col
    mine = lax.dynamic_slice_in_dim(first, z * share, share, 0)
    gram = lax.dot_general(mine, mine, TN, preferred_element_type=jnp.float32)
    wires = (jnp.float32, jnp.bfloat16, jnp.float32)
    bits = lax.axis_size("row").bit_length() - 1
    for j in range(middle, n_col):
        live, gram = lax.optimization_barrier((counts, gram))
        back = backward(tiles, col_index, live, sums[j:j + 1], sketch.shape[0], j * chunk, back)
        if j - middle < bits:
            gram = row_step(gram, j - middle, jnp.float32)
        gram, back = lax.optimization_barrier((gram, back))
    part = row_step(back, 0, wires[0])
    for k in range(min(n_col - middle, bits), bits):
        gram = row_step(gram, k, jnp.float32)
    gram = col_sum(gram)
    gram, part = lax.optimization_barrier((gram, part))
    if bits > 1:
        part = row_step(part, 1, wires[1])
    gram = row_gather(gram)
    gram, part = lax.optimization_barrier((gram, part))
    for k in range(2, bits):
        part = row_step(part, k, wires[2])
    unused, inverse = cholesky(gram, 1.0 / total_rows)
    part = lax.dot_general(part, inverse, NT, precision=HI, preferred_element_type=jnp.float32)
    back = row_gather(part.astype(jnp.bfloat16))
    back = pltpu.with_memory_space_constraint(back, pltpu.VMEM)

    parts = [
        forward(tiles, col_index, counts, back, share_order(k) * chunk, chunk) for k in range(n_col)
    ]
    second = line_scatter([part for part, _ in parts], parts[0][1])
    gram = lax.dot_general(second, second, TN, precision=HI, preferred_element_type=jnp.float32)
    factor, inverse = cholesky(gram_sum(gram), 1.0 / total_rows)
    basis = lax.dot_general(second, inverse, NT, precision=HI, preferred_element_type=jnp.float32)
    return (basis, factor)


def solution(mesh):
    return jax.shard_map(
        local,
        mesh=mesh,
        in_specs=(P("row", "col", None, None), P("row", "col"), P("row", "col"), P("col", None)),
        out_specs=(P(("row", "col"), None), P()),
        check_vma=False,
    )
```
